256 devices in a mesh: loop: 16 (over z, x_lo), row: 4 (over x_hi, core), col: 4 (over y).
Axes of the slice: x: 4 (x_hi: 2, x_lo: 2; x = x_hi * 2 + x_lo), y: 4, z: 8, core: 2. Of those that a mesh axis runs over, the one named last changes fastest.
Arguments:
- interval_blocks: bfloat16 [16, 4, 2048, 2048], P('loop', None, 'row', 'col'), may hold values from -0.15625 to 0.15625
- interval_pivots: int32 [16, 3, 2048], P('loop'), may hold values from 0 to 2047, each once within a row
- boundary_pivots: int32 [16, 2048], replicated, may hold values from 0 to 2047, each once within a row
- interval_residuals: bfloat16 [16, 4, 2048], P('loop', None, ('row', 'col')), may hold values from -0.23925781 to 0.23925781
Outputs:
- reduced_block: bfloat16 [16, 2048, 2048], P('loop', 'row', 'col')
- reduced_rhs: float32 [16, 2048], P('loop', ('row', 'col'))
The draws below stay inside these ranges and needn't reach their ends.
Inputs may be any that keep to these rules, and one draw needn't show every extreme that they name: Each row of interval_pivots is a permutation of 0 to 2047. Each row of boundary_pivots is a permutation of 0 to 2047.
All inputs are finite; a program needn't handle non-finite values.
Results may differ from the reference program's by a relative error of at most 0.018.
Values may be sent and summed in bfloat16 or wider, within the bound.
A program may use at most 64 MiB of HBM per device.

```python
import jax
import jax.numpy as jnp
from jax import lax

STATE = 2048
INTERVALS = 4
POSITIONS = 16


def block_levels(rng, shape, split, low, high):
    def one(dim, shards_of):
        draws = jax.random.uniform(jax.random.fold_in(jax.random.fold_in(rng, 6), dim), (shards_of,), jnp.float32, low / len(split), high / len(split))
        return jnp.repeat(jnp.exp(draws), shape[dim] // shards_of).reshape((-1,) + (1,) * (len(shape) - dim - 1))

    loudness = one(*split[0])
    for cut in split[1:]:
        loudness = loudness * one(*cut)
    return loudness


def centred(key, shape, deviation, most, split=(), dtype=jnp.bfloat16):
    loudness = block_levels(key, shape, split, -0.22, 0.18) if split else 1.0
    drawn = jax.random.normal(key, shape, jnp.float32) * deviation * loudness
    return jnp.minimum(jnp.maximum(drawn, -most), most).astype(dtype)


def setup_inputs(seed: int = 0) -> dict:
    splits = jax.random.split(jax.random.key(seed), 5)
    interval_blocks = centred(splits[0], (POSITIONS, INTERVALS, STATE, STATE), (STATE * 11 // 16) ** -0.5, 0.15625, ((0, 16), (2, 4), (3, 4)))
    interval_pivots = jax.vmap(lambda own: jax.random.permutation(own, STATE))(jax.random.split(splits[1], POSITIONS * (INTERVALS - 1))).reshape((POSITIONS, INTERVALS - 1, STATE)).astype(jnp.int32)
    boundary_pivots = jax.vmap(lambda own: jax.random.permutation(own, STATE))(jax.random.split(splits[2], POSITIONS)).reshape((POSITIONS, STATE)).astype(jnp.int32)
    interval_residuals = centred(splits[3], (POSITIONS, INTERVALS, STATE), 0.04, 0.23925781, ((0, 16), (2, 16)))
    return {"interval_blocks": interval_blocks, "interval_pivots": interval_pivots, "boundary_pivots": boundary_pivots, "interval_residuals": interval_residuals}


def compose(left_block, right_block, right_vector, pivots, added):
    permuted = jnp.take(right_block, pivots, axis=0)
    moved = jnp.take(right_vector, pivots, axis=0)
    product = jnp.dot(left_block, permuted, preferred_element_type=jnp.float32)
    applied = jnp.dot(left_block, moved, preferred_element_type=jnp.float32) + added.astype(jnp.float32)
    return product, applied


def condense(inputs):
    blocks, pivots, residuals = inputs
    matrix = blocks[0]
    vector = residuals[0]
    for interval in range(1, INTERVALS):
        product, applied = compose(blocks[interval], matrix, vector, pivots[interval - 1], residuals[interval])
        matrix = product.astype(jnp.bfloat16)
        vector = applied.astype(jnp.bfloat16)
    return matrix, vector


def level_first(inputs):
    current, current_vector, earlier, earlier_vector, pivots = inputs
    product, applied = compose(current, earlier, earlier_vector, pivots, current_vector)
    return product.astype(jnp.bfloat16), applied.astype(jnp.bfloat16)


def level_second(inputs):
    current, current_vector, earlier, earlier_vector, pivots = inputs
    product, applied = compose(current, earlier, earlier_vector, pivots, current_vector)
    return product.astype(jnp.bfloat16), applied


def reference(interval_blocks, interval_pivots, boundary_pivots, interval_residuals):
    cond_matrix, cond_vector = lax.map(condense, (interval_blocks, interval_pivots, interval_residuals))
    halved, halved_vector = lax.map(level_first, (cond_matrix, cond_vector, jnp.roll(cond_matrix, 1, axis=0), jnp.roll(cond_vector, 1, axis=0), boundary_pivots))
    reduced_block, reduced_rhs = lax.map(level_second, (halved, halved_vector, jnp.roll(halved, 2, axis=0), jnp.roll(halved_vector, 2, axis=0), jnp.roll(boundary_pivots, 1, axis=0)))
    return reduced_block, reduced_rhs
```

```python
import jax
import jax.numpy as jnp
from jax import lax
from jax.experimental import pallas as pl
from jax.experimental.pallas import tpu as pltpu
from jax.sharding import PartitionSpec as P

MESH = pl.DeviceIdType.MESH
BF, F32 = jnp.bfloat16, jnp.float32
NT = (((1,), (1,)), ((), ()))

ITEMS = (("F", 0), ("S", 0), ("F", 1), ("W", 0), ("S", 1), ("W", 1))
AHEAD = 3


def body(w_ref, ipiv_ref, bpiv_ref, res_ref, out_ref, rhs_ref, gath, own_vec, panel, perm, hot, gsend, gbuf, rbuf, gs_sem, gr_sem, ys_sem,
         yr_sem, ps_sem, pr_sem):
    loop, row, col = lax.axis_index("loop"), lax.axis_index("row"), lax.axis_index("col")
    n_loop, n_row, n_col = lax.axis_size("loop"), lax.axis_size("row"), lax.axis_size("col")
    nb = w_ref.shape[1]
    half, quarter = nb // 2, nb // 4
    share = res_ref.shape[1]

    def at(dloop=0, row_=None, dcol=0):
        return {
            "loop": lax.rem(loop + dloop + n_loop, n_loop),
            "row": row if row_ is None else row_,
            "col": lax.rem(col + dcol + n_col, n_col),
        }

    sibling = row + 1 - 2 * lax.rem(row, 2)
    across = lax.rem(row + 2, n_row)
    across_sibling = lax.rem(sibling + 2, n_row)
    slot_rows = (row, sibling, across, across_sibling)
    slot_cols = (col, lax.rem(col + n_col - 1, n_col), lax.rem(col + 2, n_col), lax.rem(col + 1, n_col))

    sends = []

    def send(src, dst, ssem, rsem, dev):
        copy = pltpu.make_async_remote_copy(
            src_ref=src, dst_ref=dst, send_sem=ssem, recv_sem=rsem, device_id=dev, device_id_type=MESH
        )
        copy.start()
        sends.append(copy)

    def arrived(dst, rsem):
        pltpu.make_async_remote_copy(
            src_ref=dst, dst_ref=dst, send_sem=rsem, recv_sem=rsem, device_id=at(), device_id_type=MESH
        ).wait_recv()

    def own_block(s):
        return w_ref.at[s + 1] if s < 3 else gath.at[s, 0]

    def item_refs(s, k, direction):
        kind, h = ITEMS[k]
        first = h * half + (0 if direction == 0 else quarter)
        second = h * half + (quarter if direction == 0 else 0)
        near = 1 if direction == 0 else 3
        if kind == "W":
            return gath.at[s, near, pl.ds(first, quarter)], gath.at[s, 2, pl.ds(first, quarter)]
        rows = first if kind == "F" else second
        return own_block(s).at[pl.ds(rows, quarter)], gath.at[s, near, pl.ds(rows, quarter)]

    def y_issue(s, k):
        for direction in (0, 1):
            src, dst = item_refs(s, k, direction)
            send(src, dst, ys_sem.at[s, k, direction], yr_sem.at[s, k, direction], at(dcol=1 if direction == 0 else -1))

    def y_recv(s, k):
        for direction in (0, 1):
            _, dst = item_refs(s, k, direction)
            arrived(dst, yr_sem.at[s, k, direction])
        s2, k2 = (s, k + AHEAD) if k + AHEAD < 6 else (s + 1, k + AHEAD - 6)
        if s2 < 3 or (s2 < 5 and s2 == s):
            y_issue(s2, k2)

    chunks = (pl.ds(0, half), pl.ds(half, half), pl.ds(nb, 16))

    def p_own(t, k):
        if t < 3:
            return panel.at[t, 0, chunks[k]]
        if k == 2:
            return own_vec.at[t - 3]
        return gath.at[t, 0, chunks[k]]

    def p_send(t, k, src, slot, dev):
        send(src, panel.at[t, slot, chunks[k]], ps_sem.at[t, slot, k], pr_sem.at[t, slot, k], dev)

    def p_recv(t, slot, k):
        arrived(panel.at[t, slot, chunks[k]], pr_sem.at[t, slot, k])

    def p_start(t, k):
        src = p_own(t, k)
        if t < 3:
            p_send(t, k, src, 1, at(row_=sibling))
            p_send(t, k, src, 2, at(row_=across))
        elif t == 3:
            p_send(t, k, src, 0, at(dloop=1))
            p_send(t, k, src, 2, at(dloop=1, row_=across))
        else:
            p_send(t, k, src, 0, at(dloop=2))

    def p_forward(t, k):
        if t >= 3:
            p_recv(t, 0, k)
            p_send(t, k, panel.at[t, 0, chunks[k]], 1, at(row_=sibling))
        if t == 4:
            p_send(t, k, panel.at[t, 0, chunks[k]], 2, at(row_=across))

    def p_forward_far(t, k):
        p_recv(t, 2, k)
        p_send(t, k, panel.at[t, 2, chunks[k]], 3, at(row_=sibling))

    def p_join(t, ks):
        for k in ks:
            p_recv(t, 1, k)
            p_recv(t, 3, k)

    def pivots(s, d):
        cols = pl.ds(pl.multiple_of(slot_cols[d] * nb, nb), nb)
        if s < 3:
            return ipiv_ref[pl.ds(s, 1), cols]
        return bpiv_ref[pl.ds(lax.rem(loop + n_loop - (s - 3), n_loop), 1), cols]

    def make_hot(s, d):
        q = pivots(s, d)
        for slot in range(4):
            iota = lax.broadcasted_iota(jnp.int32, (nb, nb), 0)
            hot[d, slot] = jnp.where(iota == q - slot_rows[slot] * nb, 1.0, 0.0).astype(BF)

    def permute(s, h, d, first=False):
        rows = pl.ds(h * half, half)
        left = (own_block(s) if d == 0 else gath.at[s, d])[rows, :]

        def one(slot, carry):
            moved = lax.dot_general(left, hot[d, slot], NT, preferred_element_type=F32).astype(BF)
            if first:
                perm[slot, rows, :] = moved
            else:
                perm[slot, rows, :] += moved
            return carry

        lax.fori_loop(0, 4, one, 0)

    def product(t, h):
        rows = pl.ds(h * half, half)
        total = jnp.dot(perm[0, rows, :], panel[t, 0, :nb, :], preferred_element_type=F32)
        for slot in range(1, 4):
            total += jnp.dot(perm[slot, rows, :], panel[t, slot, :nb, :], preferred_element_type=F32)
        return total

    def applied(t):
        total = lax.dot_general(panel[t, 0, nb:, :], perm[0], NT, preferred_element_type=F32)
        for slot in range(1, 4):
            total += lax.dot_general(panel[t, slot, nb:, :], perm[slot], NT, preferred_element_type=F32)
        return total

    def finish(s, h):
        rows = pl.ds(h * half, half)
        value = product(s, h).astype(BF)
        if s < 2:
            panel[s + 1, 0, rows, :] = value
        elif s < 4:
            gath[s + 1, 0, rows, :] = value
        else:
            out_ref[rows, :] = value

    def finish_vector(s):
        value = applied(s)
        if s < 3:
            value = (value + gbuf[pl.ds(s + 1, 1), :]).astype(BF)
        else:
            value = value + own_vec[s - 3].astype(F32)
        if s < 2:
            panel[s + 1, 0, nb:, :] = value
        elif s < 4:
            own_vec[s - 2] = value.astype(BF)
        else:
            rbuf[...] = value[:8, :]
            rhs_ref[...] = rbuf[pl.ds(0, 1), pl.ds(pl.multiple_of(col * share, share), share)]

    barrier = pltpu.get_barrier_semaphore()
    partners = (
        at(dcol=1), at(dcol=-1), at(dcol=2), at(row_=sibling), at(row_=across),
        at(dloop=1), at(dloop=-1), at(dloop=1, row_=across), at(dloop=-1, row_=across), at(dloop=2), at(dloop=-2),
    )
    for partner in partners:
        pl.semaphore_signal(barrier, inc=1, device_id=partner, device_id_type=MESH)
    panel[0, 0, :nb, :] = w_ref[0]
    own_cols = pl.ds(pl.multiple_of(col * share, share), share)
    gsend[...] = jnp.zeros_like(gsend)
    gsend[pl.ds(0, 4), pl.ds(0, share)] = res_ref[...].astype(F32)
    gbuf[:, own_cols] = gsend[:, pl.ds(0, share)]
    pl.semaphore_wait(barrier, len(partners))

    for k in range(AHEAD):
        y_issue(0, k)
    for k in (0, 1):
        p_start(0, k)
    for i, dcol in enumerate((1, -1, 2)):
        send(gsend.at[:, pl.ds(0, share)], gbuf.at[:, own_cols], gs_sem.at[i], gr_sem.at[i], at(dcol=dcol))
    make_hot(0, 0)
    permute(0, 0, 0, True)
    permute(0, 1, 0, True)
    make_hot(0, 1)
    make_hot(0, 3)
    for i, dcol in enumerate((-1, 1, 2)):
        arrived(gbuf.at[:, pl.ds(pl.multiple_of(lax.rem(col + dcol + n_col, n_col) * share, share), share)], gr_sem.at[i])
    panel[0, 0, nb:, :] = jnp.broadcast_to(gbuf[pl.ds(0, 1), :], (16, nb)).astype(BF)
    p_start(0, 2)

    for s in range(5):
        y_recv(s, 0)
        y_recv(s, 1)
        permute(s, 0, 1)
        permute(s, 0, 3)
        if s == 0:
            make_hot(0, 2)
        if s >= 3:
            p_forward(s, 0)
        if s < 4:
            p_forward_far(s, 0)
        y_recv(s, 2)
        y_recv(s, 3)
        permute(s, 0, 2)
        if s < 3:
            p_forward_far(s, 1)
            p_forward_far(s, 2)
            p_join(s, (0, 1, 2))
            finish(s, 0)
            p_start(s + 1, 0)
            if s == 2:
                y_issue(3, 0)
                y_issue(3, 1)
        y_recv(s, 4)
        permute(s, 1, 1)
        permute(s, 1, 3)
        if s >= 3:
            if s == 4:
                p_forward_far(s, 0)
            for k in (1, 2):
                p_forward(s, k)
                p_forward_far(s, k)
            p_join(s, (0, 1, 2))
            finish(s, 0)
            if s == 3:
                p_start(4, 0)
                y_issue(4, 0)
                y_issue(4, 1)
        y_recv(s, 5)
        permute(s, 1, 2)
        finish(s, 1)
        if s < 4:
            p_start(s + 1, 1)
            if s >= 2:
                y_issue(s + 1, 2)
        finish_vector(s)
        if s < 4:
            p_start(s + 1, 2)
            for d in (0, 1, 3, 2):
                make_hot(s + 1, d)
                if d == 0:
                    permute(s + 1, 0, 0, True)
                    permute(s + 1, 1, 0, True)
    for copy in sends:
        copy.wait_send()


def shards(interval_blocks, interval_pivots, boundary_pivots, interval_residuals):
    blocks, pivots, residuals = interval_blocks[0], interval_pivots[0], interval_residuals[0]
    nb, share = blocks.shape[1], residuals.shape[1]
    vmem = pl.BlockSpec(memory_space=pltpu.VMEM)
    reduced, rhs = pl.pallas_call(
        body,
        out_shape=(jax.ShapeDtypeStruct((nb, nb), BF), jax.ShapeDtypeStruct((1, share), F32)),
        in_specs=[vmem] * 4,
        out_specs=(vmem, vmem),
        scratch_shapes=[
            pltpu.VMEM((5, 4, nb, nb), BF),
            pltpu.VMEM((2, 16, nb), BF),
            pltpu.VMEM((5, 4, nb + 16, nb), BF),
            pltpu.VMEM((4, nb, nb), BF),
            pltpu.VMEM((4, 4, nb, nb), BF),
            pltpu.VMEM((8, nb), F32),
            pltpu.VMEM((8, nb), F32),
            pltpu.VMEM((8, nb), F32),
            pltpu.SemaphoreType.DMA((3,)),
            pltpu.SemaphoreType.DMA((3,)),
            pltpu.SemaphoreType.DMA((5, 6, 2)),
            pltpu.SemaphoreType.DMA((5, 6, 2)),
            pltpu.SemaphoreType.DMA((5, 4, 3)),
            pltpu.SemaphoreType.DMA((5, 4, 3)),
        ],
        compiler_params=pltpu.CompilerParams(
            collective_id=0, has_side_effects=True, vmem_limit_bytes=60 * 2**20
        ),
        name="newton",
    )(blocks, pivots, boundary_pivots, residuals)
    return reduced[None], rhs


def solution(mesh):
    placed = (
        P("loop", None, "row", "col"),
        P("loop", None, None),
        P(),
        P("loop", None, ("row", "col")),
    )
    return jax.shard_map(
        shards,
        mesh=mesh,
        in_specs=placed,
        out_specs=(P("loop", "row", "col"), P("loop", ("row", "col"))),
        check_vma=False,
    )
```

```python
import jax
import jax.numpy as jnp
from jax import lax
from jax.experimental import pallas as pl
from jax.experimental.pallas import tpu as pltpu
from jax.sharding import PartitionSpec as P

MESH = pl.DeviceIdType.MESH
BF, F32 = jnp.bfloat16, jnp.float32
NT = (((1,), (1,)), ((), ()))

FIRST, SECOND, PASSED = 0, 1, 2
STAGES, HALVES, VECTOR = 5, 10, 4


def body(w_ref, ipiv_ref, bpiv_ref, res_ref, out_ref, rhs_ref, gath, panel, vecs, own_vec, relay, relay_vec, perm, hot, pivs,
         gsend, gbuf, rbuf, load_sem, gs_sem, gr_sem, ys_sem, yr_sem, ps_sem, pr_sem, rs_sem, rr_sem, fs_sem):
    loop, row, col = lax.axis_index("loop"), lax.axis_index("row"), lax.axis_index("col")
    n_loop, n_row, n_col = lax.axis_size("loop"), lax.axis_size("row"), lax.axis_size("col")
    nb = perm.shape[0]
    half, quarter = nb // 2, nb // 4
    share = res_ref.shape[1]
    odd = lax.rem(loop, 2) == 1
    even = lax.rem(loop, 2) == 0
    own_lanes = pl.ds(0, nb)

    def at(dloop=0, row_=None, dcol=0):
        return {
            "loop": lax.rem(loop + dloop + n_loop, n_loop),
            "row": row if row_ is None else row_,
            "col": lax.rem(col + dcol + n_col, n_col),
        }

    sibling = row + 1 - 2 * lax.rem(row, 2)
    across = lax.rem(row + 2, n_row)

    def copy(src, dst, ssem, rsem, dev):
        return pltpu.make_async_remote_copy(
            src_ref=src, dst_ref=dst, send_sem=ssem, recv_sem=rsem, device_id=dev, device_id_type=MESH
        )

    def y_copy(j, k, direction):
        s, h = lax.div(j, 2), lax.rem(j, 2)
        near = 1 + direction
        offset = (direction + (k == SECOND)) % 2 * quarter
        rows = pl.ds(pl.multiple_of(h * half + offset, quarter), quarter)
        near_lanes = pl.ds(near * nb, nb)
        if k == PASSED:
            src, dst = gath.at[s, rows, near_lanes], gath.at[s, rows, pl.ds(3 * nb, nb)]
        else:
            src, dst = gath.at[s, rows, own_lanes], gath.at[s, rows, near_lanes]
        return copy(src, dst, ys_sem.at[j, k, direction], yr_sem.at[j, k, direction], at(dcol=1 - 2 * direction))

    def y_issue(j, k):
        for direction in (0, 1):
            y_copy(j, k, direction).start()

    def y_recv(j, k):
        for direction in (0, 1):
            y_copy(j, k, direction).wait_recv()

    def part(t, slot, q):
        if q == VECTOR:
            return vecs.at[t, :, pl.ds(slot * nb, nb)]
        return panel.at[t, pl.ds(slot * nb + q * quarter, quarter)]

    def own_part(t, q):
        if q == VECTOR:
            return own_vec.at[t - 3]
        return gath.at[t, pl.ds(q * quarter, quarter), own_lanes]

    def p_copy(t, q, src, slot, dev):
        return copy(src, part(t, slot, q), ps_sem.at[t, slot, q], pr_sem.at[t, slot, q], dev)

    def local_sends(t, q):
        return [p_copy(t, q, part(t, 0, q), 1, at(row_=sibling)), p_copy(t, q, part(t, 0, q), 2, at(row_=across))]

    def next_sends(q):
        src = own_part(3, q)
        return [p_copy(3, q, src, 0, at(dloop=1)), p_copy(3, q, src, 2, at(dloop=1, row_=across))]

    def relay_part(q):
        return relay_vec if q == VECTOR else relay.at[pl.ds(q * quarter, quarter)]

    def relay_send(q):
        return copy(own_part(3, q), relay_part(q), rs_sem.at[q], rr_sem.at[q], at(dloop=2))

    def relay_passes(q):
        src = relay_part(q)
        return [p_copy(3, q, src, 0, at(dloop=-1)), p_copy(3, q, src, 2, at(dloop=-1, row_=across))]

    def far_send(q):
        return p_copy(4, q, own_part(4, q), 0, at(dloop=2))

    def to_sibling(t, q, slot):
        return copy(part(t, slot, q), part(t, slot + 1, q), fs_sem.at[t, slot // 2, q], pr_sem.at[t, slot + 1, q], at(row_=sibling))

    def p_recv(t, slot, q):
        p_copy(t, q, part(t, slot, q), slot, at(row_=sibling)).wait_recv()

    def far_forward(t, q):
        p_recv(t, 2, q)
        to_sibling(t, q, 2).start()

    def join(t):
        for q in range(5):
            p_recv(t, 1, q)
            p_recv(t, 3, q)

    def start_next(q):
        @pl.when(even)
        def _():
            for c in next_sends(q):
                c.start()

        @pl.when(odd)
        def _():
            relay_send(q).start()

    def pass_relay(qs):
        @pl.when(odd)
        def _():
            for q in qs:
                relay_send(q).wait_recv()
                for c in relay_passes(q):
                    c.start()

    def make_hot(s):
        for slot, dcol in enumerate((0, n_col - 1, 1, 2)):
            start = pl.multiple_of(lax.rem(col + dcol, n_col) * nb, nb)
            q = pivs[pl.ds(s, 1), pl.ds(start, nb)]

            def one(row_slot, carry):
                base = lax.rem(row + 2 * lax.div(row_slot, 2), n_row)
                base = base + (1 - 2 * lax.rem(base, 2)) * lax.rem(row_slot, 2)
                iota = lax.broadcasted_iota(jnp.int32, (nb, nb), 0)
                rows = pl.ds(pl.multiple_of(row_slot * nb, nb), nb)
                hot[rows, pl.ds(slot * nb, nb)] = jnp.where(iota == q - base * nb, 1.0, 0.0).astype(BF)
                return carry

            lax.fori_loop(0, 4, one, 0)

    def permute(j, lanes, first):
        s, h = lax.div(j, 2), lax.rem(j, 2)
        rows = pl.ds(pl.multiple_of(h * half, half), half)

        def one(part_, carry):
            targets = pl.ds(pl.multiple_of(part_ * 2 * nb, 2 * nb), 2 * nb)
            moved = lax.dot_general(gath[s, rows, lanes], hot[targets, lanes], NT, preferred_element_type=F32).astype(BF)
            if first:
                perm[rows, targets] = moved
            else:
                perm[rows, targets] += moved
            return carry

        lax.fori_loop(0, 2, one, 0)

    def product(s, h):
        rows = pl.ds(pl.multiple_of(h * half, half), half)
        value = jnp.dot(perm[rows, :], panel[s], preferred_element_type=F32).astype(BF)

        @pl.when(s < 2)
        def _():
            panel[s + 1, rows, :] = value

        @pl.when((s >= 2) & (s < 4))
        def _():
            gath[s + 1, rows, own_lanes] = value

        @pl.when(s == 4)
        def _():
            out_ref[rows, :] = value

    def finish_vector(s):
        rbuf[...] = lax.dot_general(vecs[s], perm[...], NT, preferred_element_type=F32)

        @pl.when(s < 3)
        def _():
            rbuf[...] += gbuf[pl.ds(s + 1, 1), :]

        @pl.when(s >= 3)
        def _():
            rbuf[...] += own_vec[s - 3].astype(F32)

        @pl.when(s < 2)
        def _():
            vecs[s + 1, :, own_lanes] = rbuf[...].astype(BF)

        @pl.when((s >= 2) & (s < 4))
        def _():
            own_vec[s - 2] = rbuf[...].astype(BF)

    loads = [pltpu.make_async_copy(w_ref.at[0], panel.at[0, pl.ds(0, nb)], load_sem.at[0])]
    for s in range(3):
        loads.append(pltpu.make_async_copy(w_ref.at[s + 1], gath.at[s, :, own_lanes], load_sem.at[s + 1]))
    for load in loads:
        load.start()
    barrier = pltpu.get_barrier_semaphore()
    partners = (
        at(dcol=1), at(dcol=-1), at(dcol=2), at(row_=sibling), at(row_=across),
        at(dloop=1), at(dloop=-1), at(dloop=1, row_=across), at(dloop=-1, row_=across), at(dloop=2), at(dloop=-2),
    )
    for partner in partners:
        pl.semaphore_signal(barrier, inc=1, device_id=partner, device_id_type=MESH)
    own_cols = pl.ds(pl.multiple_of(col * share, share), share)
    gsend[...] = jnp.zeros_like(gsend)
    gsend[pl.ds(0, 4), :] = res_ref[...].astype(F32)
    gbuf[:, own_cols] = gsend[...]
    pivs[pl.ds(0, 3), :] = ipiv_ref[...]
    pivs[pl.ds(3, 1), :] = bpiv_ref[pl.ds(loop, 1), :]
    pivs[pl.ds(4, 1), :] = bpiv_ref[pl.ds(lax.rem(loop + n_loop - 1, n_loop), 1), :]
    for load in loads:
        load.wait()
    pl.semaphore_wait(barrier, len(partners))

    def g_copy(i, dcol, holder):
        cols = pl.ds(pl.multiple_of(lax.rem(col + holder + n_col, n_col) * share, share), share)
        return copy(gsend, gbuf.at[:, cols], gs_sem.at[i], gr_sem.at[i], at(dcol=dcol))

    y_issue(0, FIRST)
    y_issue(0, SECOND)
    for i, dcol in enumerate((1, -1, 2)):
        g_copy(i, dcol, 0).start()
    for q in range(4):
        for c in local_sends(0, q):
            c.start()
    make_hot(0)
    for i, dcol in enumerate((-1, 1, 2)):
        g_copy(i, dcol, dcol).wait_recv()
    vecs[0, :, own_lanes] = jnp.broadcast_to(gbuf[pl.ds(0, 1), :], (16, nb)).astype(BF)
    for c in local_sends(0, VECTOR):
        c.start()

    def step(j, carry):
        s, h = lax.div(j, 2), lax.rem(j, 2)
        y_recv(j, FIRST)
        y_issue(j, PASSED)
        y_recv(j, SECOND)

        @pl.when(j < 5)
        def _():
            y_issue(j + 1, FIRST)
            y_issue(j + 1, SECOND)

        permute(j, pl.ds(0, 3 * nb), True)

        @pl.when((h == 1) & (s < 2))
        def _():
            for q in (0, 1):
                far_forward(s + 1, q)

        @pl.when(j == 0)
        def _():
            for q in (0, 1):
                far_forward(0, q)

        @pl.when((h == 0) & (s < 3))
        def _():
            for q in (2, 3, VECTOR):
                far_forward(s, q)

        @pl.when(j == 5)
        def _():
            pass_relay((0, 1))

        @pl.when(j == 6)
        def _():
            pass_relay((2, 3, VECTOR))
            for q in (0, 1):
                p_recv(3, 0, q)
                to_sibling(3, q, 0).start()
                far_forward(3, q)

        @pl.when(j == 7)
        def _():
            for q in (2, 3, VECTOR):
                p_recv(3, 0, q)
                to_sibling(3, q, 0).start()
                far_forward(3, q)
            join(3)

        def receive_far(q):
            p_recv(4, 0, q)
            for c in local_sends(4, q):
                c.start()

        @pl.when(j == 8)
        def _():
            for q in (0, 1):
                receive_far(q)

        @pl.when(j == 9)
        def _():
            for q in (2, 3, VECTOR):
                receive_far(q)
            for q in range(5):
                far_forward(4, q)
            join(4)

        @pl.when((h == 1) & (s >= 3))
        def _():
            product(s, 0)

        @pl.when(j == 7)
        def _():
            for q in (0, 1):
                far_send(q).start()
            y_issue(8, FIRST)
            y_issue(8, SECOND)

        y_recv(j, PASSED)
        permute(j, pl.ds(3 * nb, nb), False)

        @pl.when((h == 0) & (s < 3))
        def _():
            join(s)

        @pl.when((h == 1) | (s < 3))
        def _():
            product(s, h)

        @pl.when((j == 4) | (j == 5) | (j == 7))
        def _():
            y_issue(j + 2, FIRST)
            y_issue(j + 2, SECOND)

        for hh in (0, 1):
            @pl.when((h == hh) & (s < 2))
            def _():
                for q in (2 * hh, 2 * hh + 1):
                    for c in local_sends(s + 1, q):
                        c.start()

            @pl.when((h == hh) & (s == 2))
            def _():
                for q in (2 * hh, 2 * hh + 1):
                    start_next(q)

        @pl.when(j == 7)
        def _():
            for q in (2, 3):
                far_send(q).start()

        @pl.when(h == 1)
        def _():
            finish_vector(s)

        @pl.when((h == 1) & (s < 2))
        def _():
            for c in local_sends(s + 1, VECTOR):
                c.start()

        @pl.when(j == 5)
        def _():
            start_next(VECTOR)

        @pl.when(j == 7)
        def _():
            far_send(VECTOR).start()

        @pl.when((h == 1) & (s < 4))
        def _():
            make_hot(s + 1)

        return carry

    lax.fori_loop(0, HALVES, step, 0)
    rhs_ref[...] = rbuf[pl.ds(0, 1), own_cols]

    for i, dcol in enumerate((1, -1, 2)):
        g_copy(i, dcol, 0).wait_send()

    def drain(j, carry):
        for k in (FIRST, SECOND, PASSED):
            for direction in (0, 1):
                y_copy(j, k, direction).wait_send()
        return carry

    lax.fori_loop(0, HALVES, drain, 0)

    def drain_panel(t, carry):
        for q in range(5):
            for c in local_sends(t, q):
                c.wait_send()
            to_sibling(t, q, 2).wait_send()
        return carry

    lax.fori_loop(0, 3, drain_panel, 0)
    drain_panel(4, 0)
    for q in range(5):
        far_send(q).wait_send()
        to_sibling(3, q, 0).wait_send()
        to_sibling(3, q, 2).wait_send()
        for c in next_sends(q):
            c.wait_send()

    @pl.when(odd)
    def _():
        for q in range(5):
            relay_send(q).wait_send()


def shards(interval_blocks, interval_pivots, boundary_pivots, interval_residuals):
    blocks, pivots, residuals = interval_blocks[0], interval_pivots[0], interval_residuals[0]
    nb, share = blocks.shape[1], residuals.shape[1]
    vmem = pl.BlockSpec(memory_space=pltpu.VMEM)
    reduced, rhs = pl.pallas_call(
        body,
        out_shape=(jax.ShapeDtypeStruct((nb, nb), BF), jax.ShapeDtypeStruct((1, share), F32)),
        in_specs=[pl.BlockSpec(memory_space=pl.ANY)] + [vmem] * 3,
        out_specs=(vmem, vmem),
        scratch_shapes=[
            pltpu.VMEM((STAGES, nb, 4 * nb), BF),
            pltpu.VMEM((STAGES, 4 * nb, nb), BF),
            pltpu.VMEM((STAGES, 16, 4 * nb), BF),
            pltpu.VMEM((2, 16, nb), BF),
            pltpu.VMEM((nb, nb), BF),
            pltpu.VMEM((16, nb), BF),
            pltpu.VMEM((nb, 4 * nb), BF),
            pltpu.VMEM((4 * nb, 4 * nb), BF),
            pltpu.VMEM((8, 4 * nb), jnp.int32),
            pltpu.VMEM((8, share), F32),
            pltpu.VMEM((8, nb), F32),
            pltpu.VMEM((16, nb), F32),
            pltpu.SemaphoreType.DMA((4,)),
            pltpu.SemaphoreType.DMA((3,)),
            pltpu.SemaphoreType.DMA((3,)),
            pltpu.SemaphoreType.DMA((HALVES, 3, 2)),
            pltpu.SemaphoreType.DMA((HALVES, 3, 2)),
            pltpu.SemaphoreType.DMA((STAGES, 4, 5)),
            pltpu.SemaphoreType.DMA((STAGES, 4, 5)),
            pltpu.SemaphoreType.DMA((5,)),
            pltpu.SemaphoreType.DMA((5,)),
            pltpu.SemaphoreType.DMA((STAGES, 2, 5)),
        ],
        compiler_params=pltpu.CompilerParams(
            collective_id=0, has_side_effects=True, vmem_limit_bytes=60 * 2**20
        ),
        name="newton",
    )(blocks, pivots, boundary_pivots, residuals)
    return reduced[None], rhs


def solution(mesh):
    placed = (
        P("loop", None, "row", "col"),
        P("loop", None, None),
        P(),
        P("loop", None, ("row", "col")),
    )
    return jax.shard_map(
        shards,
        mesh=mesh,
        in_specs=placed,
        out_specs=(P("loop", "row", "col"), P("loop", ("row", "col"))),
        check_vma=False,
    )
```

```python
import jax
import jax.numpy as jnp
from jax import lax
from jax.experimental import pallas as pl
from jax.experimental.pallas import tpu as pltpu
from jax.sharding import PartitionSpec as P

MESH = pl.DeviceIdType.MESH
BF, F32 = jnp.bfloat16, jnp.float32
NT = (((1,), (1,)), ((), ()))

FIRST, SECOND, PASSED = 0, 1, 2
STAGES, HALVES, VECTOR = 5, 10, 4


def body(w_ref, ipiv_ref, bpiv_ref, res_ref, out_ref, rhs_ref, gath, panel, vecs, own_vec, relay, relay_vec, perm, hot, pivs,
         gsend, gbuf, rbuf, held, load_sem, gs_sem, gr_sem, ys_sem, yr_sem, ps_sem, pr_sem, rs_sem, rr_sem, fs_sem):
    loop, row, col = lax.axis_index("loop"), lax.axis_index("row"), lax.axis_index("col")
    n_loop, n_row, n_col = lax.axis_size("loop"), lax.axis_size("row"), lax.axis_size("col")
    nb = perm.shape[0]
    half, quarter = nb // 2, nb // 4
    share = res_ref.shape[1]
    odd = lax.rem(loop, 2) == 1
    even = lax.rem(loop, 2) == 0
    own_lanes = pl.ds(0, nb)

    def at(dloop=0, row_=None, dcol=0):
        return {
            "loop": lax.rem(loop + dloop + n_loop, n_loop),
            "row": row if row_ is None else row_,
            "col": lax.rem(col + dcol + n_col, n_col),
        }

    sibling = row + 1 - 2 * lax.rem(row, 2)
    across = lax.rem(row + 2, n_row)

    def copy(src, dst, ssem, rsem, dev):
        return pltpu.make_async_remote_copy(
            src_ref=src, dst_ref=dst, send_sem=ssem, recv_sem=rsem, device_id=dev, device_id_type=MESH
        )

    def y_copy(j, k, direction):
        s, h = lax.div(j, 2), lax.rem(j, 2)
        near = 1 + direction
        offset = (direction + (k == SECOND)) % 2 * quarter
        rows = pl.ds(pl.multiple_of(h * half + offset, quarter), quarter)
        near_lanes = pl.ds(near * nb, nb)
        if k == PASSED:
            src, dst = gath.at[s, rows, near_lanes], gath.at[s, rows, pl.ds(3 * nb, nb)]
        else:
            src, dst = gath.at[s, rows, own_lanes], gath.at[s, rows, near_lanes]
        return copy(src, dst, ys_sem.at[j, k, direction], yr_sem.at[j, k, direction], at(dcol=1 - 2 * direction))

    def y_issue(j, k):
        for direction in (0, 1):
            y_copy(j, k, direction).start()

    def y_recv(j, k):
        for direction in (0, 1):
            y_copy(j, k, direction).wait_recv()

    def part(t, slot, q):
        if q == VECTOR:
            return vecs.at[t, :, pl.ds(slot * nb, nb)]
        return panel.at[t, pl.ds(slot * nb + q * quarter, quarter)]

    def own_part(t, q):
        if q == VECTOR:
            return own_vec.at[t - 3]
        return gath.at[t, pl.ds(q * quarter, quarter), own_lanes]

    def p_copy(t, q, src, slot, dev):
        return copy(src, part(t, slot, q), ps_sem.at[t, slot, q], pr_sem.at[t, slot, q], dev)

    def local_sends(t, q):
        return [p_copy(t, q, part(t, 0, q), 1, at(row_=sibling)), p_copy(t, q, part(t, 0, q), 2, at(row_=across))]

    def next_sends(q):
        src = own_part(3, q)
        return [p_copy(3, q, src, 0, at(dloop=1)), p_copy(3, q, src, 2, at(dloop=1, row_=across))]

    def relay_part(q):
        return relay_vec if q == VECTOR else relay.at[pl.ds(q * quarter, quarter)]

    def relay_send(q):
        return copy(own_part(3, q), relay_part(q), rs_sem.at[q], rr_sem.at[q], at(dloop=2))

    def relay_passes(q):
        src = relay_part(q)
        return [p_copy(3, q, src, 0, at(dloop=-1)), p_copy(3, q, src, 2, at(dloop=-1, row_=across))]

    def far_send(q):
        return p_copy(4, q, own_part(4, q), 0, at(dloop=2))

    def to_sibling(t, q, slot):
        return copy(part(t, slot, q), part(t, slot + 1, q), fs_sem.at[t, slot // 2, q], pr_sem.at[t, slot + 1, q], at(row_=sibling))

    def p_recv(t, slot, q):
        p_copy(t, q, part(t, slot, q), slot, at(row_=sibling)).wait_recv()

    def far_forward(t, q):
        p_recv(t, 2, q)
        to_sibling(t, q, 2).start()

    def join(t):
        for q in range(5):
            p_recv(t, 1, q)
            p_recv(t, 3, q)

    def start_next(q):
        @pl.when(even)
        def _():
            for c in next_sends(q):
                c.start()

        @pl.when(odd)
        def _():
            relay_send(q).start()

    def pass_relay(qs):
        @pl.when(odd)
        def _():
            for q in qs:
                relay_send(q).wait_recv()
                for c in relay_passes(q):
                    c.start()

    def make_hot(s):
        for slot, dcol in enumerate((0, n_col - 1, 1, 2)):
            start = pl.multiple_of(lax.rem(col + dcol, n_col) * nb, nb)
            q = pivs[pl.ds(s, 1), pl.ds(start, nb)]

            def one(row_slot, carry):
                base = lax.rem(row + 2 * lax.div(row_slot, 2), n_row)
                base = base + (1 - 2 * lax.rem(base, 2)) * lax.rem(row_slot, 2)
                iota = lax.broadcasted_iota(jnp.int32, (nb, nb), 0)
                rows = pl.ds(pl.multiple_of(row_slot * nb, nb), nb)
                hot[rows, pl.ds(slot * nb, nb)] = jnp.where(iota == q - base * nb, 1.0, 0.0).astype(BF)
                return carry

            lax.fori_loop(0, 4, one, 0)

    def permute(j, lanes, first):
        s, h = lax.div(j, 2), lax.rem(j, 2)
        rows = pl.ds(pl.multiple_of(h * half, half), half)

        def one(part_, carry):
            targets = pl.ds(pl.multiple_of(part_ * 2 * nb, 2 * nb), 2 * nb)
            moved = lax.dot_general(gath[s, rows, lanes], hot[targets, lanes], NT, preferred_element_type=F32).astype(BF)
            if first:
                perm[rows, targets] = moved
            else:
                perm[rows, targets] += moved
            return carry

        lax.fori_loop(0, 2, one, 0)

    def product(s, h):
        rows = pl.ds(pl.multiple_of(h * half, half), half)
        value = jnp.dot(perm[rows, :], panel[s], preferred_element_type=F32).astype(BF)

        @pl.when(s == 0)
        def _():
            panel[2, rows, :] = value

        @pl.when((s >= 1) & (s < 4))
        def _():
            gath[s + 1, rows, own_lanes] = value

        @pl.when(s == 4)
        def _():
            out_ref[rows, :] = value

    def finish_vector(s):
        rbuf[...] = lax.dot_general(vecs[s], perm[...], NT, preferred_element_type=F32)

        @pl.when(s < 2)
        def _():
            rbuf[...] += gbuf[pl.ds(2 * s + 1, 1), :]

        @pl.when(s == 0)
        def _():
            vecs[2, :, own_lanes] = rbuf[...].astype(BF)

        @pl.when(s == 1)
        def _():
            held[...] = rbuf[...]

        @pl.when(s == 2)
        def _():
            rbuf[...] += held[...]

        @pl.when(s >= 3)
        def _():
            rbuf[...] += own_vec[s - 3].astype(F32)

        @pl.when((s >= 2) & (s < 4))
        def _():
            own_vec[s - 2] = rbuf[...].astype(BF)

    loads = []
    for s in range(2):
        loads.append(pltpu.make_async_copy(w_ref.at[2 * s + 1], gath.at[s, :, own_lanes], load_sem.at[2 * s]))
        loads.append(pltpu.make_async_copy(w_ref.at[2 * s], panel.at[s, pl.ds(0, nb)], load_sem.at[2 * s + 1]))
    for load in loads:
        load.start()
    barrier = pltpu.get_barrier_semaphore()
    partners = (
        at(dcol=1), at(dcol=-1), at(dcol=2), at(row_=sibling), at(row_=across),
        at(dloop=1), at(dloop=-1), at(dloop=1, row_=across), at(dloop=-1, row_=across), at(dloop=2), at(dloop=-2),
    )
    for partner in partners:
        pl.semaphore_signal(barrier, inc=1, device_id=partner, device_id_type=MESH)
    own_cols = pl.ds(pl.multiple_of(col * share, share), share)
    gsend[...] = jnp.zeros_like(gsend)
    gsend[pl.ds(0, 4), :] = res_ref[...].astype(F32)
    gbuf[:, own_cols] = gsend[...]
    for s, interval in enumerate((0, 2, 1)):
        pivs[pl.ds(s, 1), :] = ipiv_ref[pl.ds(interval, 1), :]
    pivs[pl.ds(3, 1), :] = bpiv_ref[pl.ds(loop, 1), :]
    pivs[pl.ds(4, 1), :] = bpiv_ref[pl.ds(lax.rem(loop + n_loop - 1, n_loop), 1), :]
    for load in loads:
        load.wait()
    pl.semaphore_wait(barrier, len(partners))

    def g_copy(i, dcol, holder):
        cols = pl.ds(pl.multiple_of(lax.rem(col + holder + n_col, n_col) * share, share), share)
        return copy(gsend, gbuf.at[:, cols], gs_sem.at[i], gr_sem.at[i], at(dcol=dcol))

    for j in (0, 1):
        y_issue(j, FIRST)
        y_issue(j, SECOND)
    for i, dcol in enumerate((1, -1, 2)):
        g_copy(i, dcol, 0).start()
    for q in range(4):
        for c in local_sends(0, q):
            c.start()
    make_hot(0)
    for i, dcol in enumerate((-1, 1, 2)):
        g_copy(i, dcol, dcol).wait_recv()
    for s in (0, 1):
        vecs[s, :, own_lanes] = jnp.broadcast_to(gbuf[pl.ds(2 * s, 1), :], (16, nb)).astype(BF)
    for c in local_sends(0, VECTOR):
        c.start()

    def step(j, carry):
        s, h = lax.div(j, 2), lax.rem(j, 2)
        y_recv(j, FIRST)
        y_issue(j, PASSED)
        y_recv(j, SECOND)

        for last, new in ((0, 2), (2, 3)):
            @pl.when(j == last)
            def _():
                y_issue(new, FIRST)
                y_issue(new, SECOND)

        permute(j, pl.ds(0, 3 * nb), True)

        @pl.when(j == 0)
        def _():
            for q in range(5):
                far_forward(0, q)
                for c in local_sends(1, q):
                    c.start()

        @pl.when(j == 1)
        def _():
            for q in (0, 1):
                far_forward(1, q)

        @pl.when(j == 2)
        def _():
            for q in (2, 3, VECTOR):
                far_forward(1, q)

        @pl.when(j == 3)
        def _():
            for q in range(5):
                far_forward(2, q)

        @pl.when(j == 5)
        def _():
            pass_relay((0, 1))

        @pl.when(j == 6)
        def _():
            pass_relay((2, 3, VECTOR))
            for q in (0, 1):
                p_recv(3, 0, q)
                to_sibling(3, q, 0).start()
                far_forward(3, q)

        @pl.when(j == 7)
        def _():
            for q in (2, 3, VECTOR):
                p_recv(3, 0, q)
                to_sibling(3, q, 0).start()
                far_forward(3, q)
            join(3)

        def receive_far(q):
            p_recv(4, 0, q)
            for c in local_sends(4, q):
                c.start()

        @pl.when(j == 8)
        def _():
            for q in (0, 1):
                receive_far(q)

        @pl.when(j == 9)
        def _():
            for q in (2, 3, VECTOR):
                receive_far(q)
            for q in range(5):
                far_forward(4, q)
            join(4)

        @pl.when((h == 1) & (s >= 3))
        def _():
            product(s, 0)

        @pl.when(j == 7)
        def _():
            for q in (0, 1):
                far_send(q).start()
            y_issue(8, FIRST)
            y_issue(8, SECOND)

        y_recv(j, PASSED)
        permute(j, pl.ds(3 * nb, nb), False)

        @pl.when((h == 0) & (s < 3))
        def _():
            join(s)

        @pl.when((h == 1) | (s < 3))
        def _():
            product(s, h)

        @pl.when((j == 2) | (j == 3) | (j == 4) | (j == 5) | (j == 7))
        def _():
            y_issue(j + 2, FIRST)
            y_issue(j + 2, SECOND)

        for hh in (0, 1):
            @pl.when(j == hh)
            def _():
                for q in (2 * hh, 2 * hh + 1):
                    for c in local_sends(2, q):
                        c.start()

            @pl.when((h == hh) & (s == 2))
            def _():
                for q in (2 * hh, 2 * hh + 1):
                    start_next(q)

        @pl.when(j == 7)
        def _():
            for q in (2, 3):
                far_send(q).start()

        @pl.when(h == 1)
        def _():
            finish_vector(s)

        @pl.when(j == 1)
        def _():
            for c in local_sends(2, VECTOR):
                c.start()

        @pl.when(j == 5)
        def _():
            start_next(VECTOR)

        @pl.when(j == 7)
        def _():
            far_send(VECTOR).start()

        @pl.when((h == 1) & (s < 4))
        def _():
            make_hot(s + 1)

        return carry

    lax.fori_loop(0, HALVES, step, 0)
    rhs_ref[...] = rbuf[pl.ds(0, 1), own_cols]

    for i, dcol in enumerate((1, -1, 2)):
        g_copy(i, dcol, 0).wait_send()

    def drain(j, carry):
        for k in (FIRST, SECOND, PASSED):
            for direction in (0, 1):
                y_copy(j, k, direction).wait_send()
        return carry

    lax.fori_loop(0, HALVES, drain, 0)

    def drain_panel(t, carry):
        for q in range(5):
            for c in local_sends(t, q):
                c.wait_send()
            to_sibling(t, q, 2).wait_send()
        return carry

    lax.fori_loop(0, 3, drain_panel, 0)
    drain_panel(4, 0)
    for q in range(5):
        far_send(q).wait_send()
        to_sibling(3, q, 0).wait_send()
        to_sibling(3, q, 2).wait_send()
        for c in next_sends(q):
            c.wait_send()

    @pl.when(odd)
    def _():
        for q in range(5):
            relay_send(q).wait_send()


def shards(interval_blocks, interval_pivots, boundary_pivots, interval_residuals):
    blocks, pivots, residuals = interval_blocks[0], interval_pivots[0], interval_residuals[0]
    nb, share = blocks.shape[1], residuals.shape[1]
    vmem = pl.BlockSpec(memory_space=pltpu.VMEM)
    reduced, rhs = pl.pallas_call(
        body,
        out_shape=(jax.ShapeDtypeStruct((nb, nb), BF), jax.ShapeDtypeStruct((1, share), F32)),
        in_specs=[pl.BlockSpec(memory_space=pl.ANY)] + [vmem] * 3,
        out_specs=(vmem, vmem),
        scratch_shapes=[
            pltpu.VMEM((STAGES, nb, 4 * nb), BF),
            pltpu.VMEM((STAGES, 4 * nb, nb), BF),
            pltpu.VMEM((STAGES, 16, 4 * nb), BF),
            pltpu.VMEM((2, 16, nb), BF),
            pltpu.VMEM((nb, nb), BF),
            pltpu.VMEM((16, nb), BF),
            pltpu.VMEM((nb, 4 * nb), BF),
            pltpu.VMEM((4 * nb, 4 * nb), BF),
            pltpu.VMEM((8, 4 * nb), jnp.int32),
            pltpu.VMEM((8, share), F32),
            pltpu.VMEM((8, nb), F32),
            pltpu.VMEM((16, nb), F32),
            pltpu.VMEM((16, nb), F32),
            pltpu.SemaphoreType.DMA((4,)),
            pltpu.SemaphoreType.DMA((3,)),
            pltpu.SemaphoreType.DMA((3,)),
            pltpu.SemaphoreType.DMA((HALVES, 3, 2)),
            pltpu.SemaphoreType.DMA((HALVES, 3, 2)),
            pltpu.SemaphoreType.DMA((STAGES, 4, 5)),
            pltpu.SemaphoreType.DMA((STAGES, 4, 5)),
            pltpu.SemaphoreType.DMA((5,)),
            pltpu.SemaphoreType.DMA((5,)),
            pltpu.SemaphoreType.DMA((STAGES, 2, 5)),
        ],
        compiler_params=pltpu.CompilerParams(
            collective_id=0, has_side_effects=True, vmem_limit_bytes=60 * 2**20
        ),
        name="newton",
    )(blocks, pivots, boundary_pivots, residuals)
    return reduced[None], rhs


def solution(mesh):
    placed = (
        P("loop", None, "row", "col"),
        P("loop", None, None),
        P(),
        P("loop", None, ("row", "col")),
    )
    return jax.shard_map(
        shards,
        mesh=mesh,
        in_specs=placed,
        out_specs=(P("loop", "row", "col"), P("loop", ("row", "col"))),
        check_vma=False,
    )
```

```python
import jax
import jax.numpy as jnp
from jax import lax
from jax.experimental import pallas as pl
from jax.experimental.pallas import tpu as pltpu
from jax.sharding import PartitionSpec as P

MESH = pl.DeviceIdType.MESH
BF, F32 = jnp.bfloat16, jnp.float32
NT = (((1,), (1,)), ((), ()))

FIRST, SECOND, PASSED = 0, 1, 2
STAGES, HALVES, VECTOR = 5, 10, 4


def body(w_ref, ipiv_ref, bpiv_ref, res_ref, out_ref, rhs_ref, gath, panel, vecs, own_vec, relay, relay_vec, perm, hot, pivs,
         gsend, gbuf, rbuf, held, load_sem, gs_sem, gr_sem, ys_sem, yr_sem, ps_sem, pr_sem, rs_sem, rr_sem, fs_sem):
    loop, row, col = lax.axis_index("loop"), lax.axis_index("row"), lax.axis_index("col")
    n_loop, n_row, n_col = lax.axis_size("loop"), lax.axis_size("row"), lax.axis_size("col")
    nb = perm.shape[0]
    half, quarter = nb // 2, nb // 4
    share = res_ref.shape[1]
    odd = lax.rem(loop, 2) == 1
    even = lax.rem(loop, 2) == 0
    own_lanes = pl.ds(0, nb)

    def at(dloop=0, row_=None, dcol=0):
        return {
            "loop": lax.rem(loop + dloop + n_loop, n_loop),
            "row": row if row_ is None else row_,
            "col": lax.rem(col + dcol + n_col, n_col),
        }

    sibling = row + 1 - 2 * lax.rem(row, 2)
    across = lax.rem(row + 2, n_row)

    def copy(src, dst, ssem, rsem, dev):
        return pltpu.make_async_remote_copy(
            src_ref=src, dst_ref=dst, send_sem=ssem, recv_sem=rsem, device_id=dev, device_id_type=MESH
        )

    def y_copy(j, k, direction):
        s, h = lax.div(j, 2), lax.rem(j, 2)
        near = 1 + direction
        offset = (direction + (k == SECOND)) % 2 * quarter
        rows = pl.ds(pl.multiple_of(h * half + offset, quarter), quarter)
        near_lanes = pl.ds(near * nb, nb)
        if k == PASSED:
            src, dst = gath.at[s, rows, near_lanes], gath.at[s, rows, pl.ds(3 * nb, nb)]
        else:
            src, dst = gath.at[s, rows, own_lanes], gath.at[s, rows, near_lanes]
        return copy(src, dst, ys_sem.at[j, k, direction], yr_sem.at[j, k, direction], at(dcol=1 - 2 * direction))

    def y_issue(j, k):
        for direction in (0, 1):
            y_copy(j, k, direction).start()

    def y_recv(j, k):
        for direction in (0, 1):
            y_copy(j, k, direction).wait_recv()

    def part(t, slot, q):
        if q == VECTOR:
            return vecs.at[t, :, pl.ds(slot * nb, nb)]
        return panel.at[t, pl.ds(slot * nb + q * quarter, quarter)]

    def own_part(t, q):
        if q == VECTOR:
            return own_vec.at[t - 3]
        return gath.at[t, pl.ds(q * quarter, quarter), own_lanes]

    def p_copy(t, q, src, slot, dev):
        return copy(src, part(t, slot, q), ps_sem.at[t, slot, q], pr_sem.at[t, slot, q], dev)

    def local_sends(t, q):
        return [p_copy(t, q, part(t, 0, q), 1, at(row_=sibling)), p_copy(t, q, part(t, 0, q), 2, at(row_=across))]

    def next_sends(q):
        src = own_part(3, q)
        return [p_copy(3, q, src, 0, at(dloop=1)), p_copy(3, q, src, 2, at(dloop=1, row_=across))]

    def relay_part(q):
        return relay_vec if q == VECTOR else relay.at[pl.ds(q * quarter, quarter)]

    def relay_send(q):
        return copy(own_part(3, q), relay_part(q), rs_sem.at[q], rr_sem.at[q], at(dloop=2))

    def relay_passes(q):
        src = relay_part(q)
        return [p_copy(3, q, src, 0, at(dloop=-1)), p_copy(3, q, src, 2, at(dloop=-1, row_=across))]

    def far_send(q):
        return p_copy(4, q, own_part(4, q), 0, at(dloop=2))

    def to_sibling(t, q, slot):
        return copy(part(t, slot, q), part(t, slot + 1, q), fs_sem.at[t, slot // 2, q], pr_sem.at[t, slot + 1, q], at(row_=sibling))

    def p_recv(t, slot, q):
        p_copy(t, q, part(t, slot, q), slot, at(row_=sibling)).wait_recv()

    def far_forward(t, q):
        p_recv(t, 2, q)
        to_sibling(t, q, 2).start()

    def join(t):
        for q in range(5):
            p_recv(t, 1, q)
            p_recv(t, 3, q)

    def start_next(q):
        @pl.when(even)
        def _():
            for c in next_sends(q):
                c.start()

        @pl.when(odd)
        def _():
            relay_send(q).start()

    def pass_relay(q):
        @pl.when(odd)
        def _():
            relay_send(q).wait_recv()
            for c in relay_passes(q):
                c.start()

    def make_hot(s):
        for slot, dcol in enumerate((0, n_col - 1, 1, 2)):
            start = pl.multiple_of(lax.rem(col + dcol, n_col) * nb, nb)
            q = pivs[pl.ds(s, 1), pl.ds(start, nb)]

            def one(row_slot, carry):
                base = lax.rem(row + 2 * lax.div(row_slot, 2), n_row)
                base = base + (1 - 2 * lax.rem(base, 2)) * lax.rem(row_slot, 2)
                iota = lax.broadcasted_iota(jnp.int32, (nb, nb), 0)
                rows = pl.ds(pl.multiple_of(row_slot * nb, nb), nb)
                hot[rows, pl.ds(slot * nb, nb)] = jnp.where(iota == q - base * nb, 1.0, 0.0).astype(BF)
                return carry

            lax.fori_loop(0, 4, one, 0)

    def permute(j, lanes, first):
        s, h = lax.div(j, 2), lax.rem(j, 2)
        rows = pl.ds(pl.multiple_of(h * half, half), half)

        def one(part_, carry):
            targets = pl.ds(pl.multiple_of(part_ * 2 * nb, 2 * nb), 2 * nb)
            moved = lax.dot_general(gath[s, rows, lanes], hot[targets, lanes], NT, preferred_element_type=F32).astype(BF)
            if first:
                perm[rows, targets] = moved
            else:
                perm[rows, targets] += moved
            return carry

        lax.fori_loop(0, 2, one, 0)

    def product(s, h):
        rows = pl.ds(pl.multiple_of(h * half, half), half)
        value = jnp.dot(perm[rows, :], panel[s], preferred_element_type=F32).astype(BF)

        @pl.when(s == 0)
        def _():
            panel[2, rows, :] = value

        @pl.when((s >= 1) & (s < 4))
        def _():
            gath[s + 1, rows, own_lanes] = value

        @pl.when(s == 4)
        def _():
            out_ref[rows, :] = value

    def finish_vector(s):
        rbuf[...] = lax.dot_general(vecs[s], perm[...], NT, preferred_element_type=F32)

        @pl.when(s < 2)
        def _():
            rbuf[...] += gbuf[pl.ds(2 * s + 1, 1), :]

        @pl.when(s == 0)
        def _():
            vecs[2, :, own_lanes] = rbuf[...].astype(BF)

        @pl.when(s == 1)
        def _():
            held[...] = rbuf[...]

        @pl.when(s == 2)
        def _():
            rbuf[...] += held[...]

        @pl.when(s >= 3)
        def _():
            rbuf[...] += own_vec[s - 3].astype(F32)

        @pl.when((s >= 2) & (s < 4))
        def _():
            own_vec[s - 2] = rbuf[...].astype(BF)

    loads = []
    for s in range(2):
        loads.append(pltpu.make_async_copy(w_ref.at[2 * s + 1], gath.at[s, :, own_lanes], load_sem.at[2 * s]))
        loads.append(pltpu.make_async_copy(w_ref.at[2 * s], panel.at[s, pl.ds(0, nb)], load_sem.at[2 * s + 1]))
    for load in loads:
        load.start()
    barrier = pltpu.get_barrier_semaphore()
    partners = (
        at(dcol=1), at(dcol=-1), at(dcol=2), at(row_=sibling), at(row_=across),
        at(dloop=1), at(dloop=-1), at(dloop=1, row_=across), at(dloop=-1, row_=across), at(dloop=2), at(dloop=-2),
    )
    for partner in partners:
        pl.semaphore_signal(barrier, inc=1, device_id=partner, device_id_type=MESH)
    own_cols = pl.ds(pl.multiple_of(col * share, share), share)
    gsend[...] = jnp.zeros_like(gsend)
    gsend[pl.ds(0, 4), :] = res_ref[...].astype(F32)
    gbuf[:, own_cols] = gsend[...]
    for s, interval in enumerate((0, 2, 1)):
        pivs[pl.ds(s, 1), :] = ipiv_ref[pl.ds(interval, 1), :]
    pivs[pl.ds(3, 1), :] = bpiv_ref[pl.ds(loop, 1), :]
    pivs[pl.ds(4, 1), :] = bpiv_ref[pl.ds(lax.rem(loop + n_loop - 1, n_loop), 1), :]
    for load in loads:
        load.wait()
    pl.semaphore_wait(barrier, len(partners))

    def g_copy(i, dcol, holder):
        cols = pl.ds(pl.multiple_of(lax.rem(col + holder + n_col, n_col) * share, share), share)
        return copy(gsend, gbuf.at[:, cols], gs_sem.at[i], gr_sem.at[i], at(dcol=dcol))

    for j in (0, 1):
        y_issue(j, FIRST)
        y_issue(j, SECOND)
    for i, dcol in enumerate((1, -1, 2)):
        g_copy(i, dcol, 0).start()
    for q in range(4):
        for c in local_sends(0, q):
            c.start()
    make_hot(0)
    for i, dcol in enumerate((-1, 1, 2)):
        g_copy(i, dcol, dcol).wait_recv()
    for s in (0, 1):
        vecs[s, :, own_lanes] = jnp.broadcast_to(gbuf[pl.ds(2 * s, 1), :], (16, nb)).astype(BF)
    for c in local_sends(0, VECTOR):
        c.start()

    def step(j, carry):
        s, h = lax.div(j, 2), lax.rem(j, 2)

        def on(number, *actions):
            @pl.when(j == number)
            def _():
                for action, qs in actions:
                    for q in qs:
                        action(q)

        def first_far(q):
            far_forward(0, q)
            for c in local_sends(1, q):
                c.start()

        def second_far(q):
            far_forward(1, q)

        def third_far(q):
            far_forward(2, q)

        def pass_next(q):
            for slot in (0, 2):
                p_recv(3, slot, q)
                to_sibling(3, q, slot).start()

        def receive_far(q):
            p_recv(4, 0, q)
            for c in local_sends(4, q):
                c.start()

        def last_far(q):
            far_forward(4, q)

        y_recv(j, FIRST)
        y_issue(j, PASSED)
        on(6, (pass_relay, (1,)), (pass_next, (0,)))
        on(8, (receive_far, (0,)))

        @pl.when((h == 0) & (s > 0))
        def _():
            make_hot(s)

        on(8, (receive_far, (1,)))
        y_recv(j, SECOND)
        for last, new in ((0, 2), (2, 3)):
            @pl.when(j == last)
            def _():
                y_issue(new, FIRST)
                y_issue(new, SECOND)

        on(6, (pass_next, (1,)), (pass_relay, (2,)))
        on(7, (pass_next, (2,)))
        on(9, (last_far, (1, 2)))
        permute(j, pl.ds(0, 3 * nb), True)
        on(0, (first_far, (0, 1, 2, 3, VECTOR)))
        on(1, (second_far, (0, 1)))
        on(2, (second_far, (2, 3, VECTOR)))
        on(3, (third_far, (0, 1, 2, 3, VECTOR)))
        on(5, (pass_relay, (0,)))
        on(6, (pass_relay, (3, VECTOR)))
        on(7, (pass_next, (3, VECTOR)))
        on(8, (receive_far, (2,)))
        on(9, (last_far, (3, VECTOR)))
        y_recv(j, PASSED)
        permute(j, pl.ds(3 * nb, nb), False)
        on(8, (receive_far, (3, VECTOR)), (last_far, (0,)))

        @pl.when((h == 0) & (s < 3))
        def _():
            join(s)

        on(7, (join, (3,)))
        on(9, (join, (4,)))

        def multiply(hh, carry):
            product(s, hh)
            return carry

        low = jnp.where(s < 3, h, 0)
        high = jnp.where((s < 3) | (h == 1), h + 1, 0)
        lax.fori_loop(low, high, multiply, 0)

        for done, new in ((2, (4,)), (3, (5,)), (4, (6,)), (5, (7,)), (7, (8, 9))):
            @pl.when(j == done)
            def _():
                for n in new:
                    y_issue(n, FIRST)
                    y_issue(n, SECOND)

        def start_third(q):
            for c in local_sends(2, q):
                c.start()

        def start_far(q):
            far_send(q).start()

        on(0, (start_third, (0, 1)))
        on(1, (start_third, (2, 3)))
        on(4, (start_next, (0, 1)))
        on(5, (start_next, (2, 3)))
        on(7, (start_far, (0, 1, 2, 3)))

        @pl.when(h == 1)
        def _():
            finish_vector(s)

        on(1, (start_third, (VECTOR,)))
        on(5, (start_next, (VECTOR,)))
        on(7, (start_far, (VECTOR,)))
        return carry

    lax.fori_loop(0, HALVES, step, 0)
    rhs_ref[...] = rbuf[pl.ds(0, 1), own_cols]

    for i, dcol in enumerate((1, -1, 2)):
        g_copy(i, dcol, 0).wait_send()

    def drain(j, carry):
        for k in (FIRST, SECOND, PASSED):
            for direction in (0, 1):
                y_copy(j, k, direction).wait_send()
        return carry

    lax.fori_loop(0, HALVES, drain, 0)

    def drain_panel(t, carry):
        for q in range(5):
            for c in local_sends(t, q):
                c.wait_send()
            to_sibling(t, q, 2).wait_send()
        return carry

    lax.fori_loop(0, 3, drain_panel, 0)
    drain_panel(4, 0)
    for q in range(5):
        far_send(q).wait_send()
        to_sibling(3, q, 0).wait_send()
        to_sibling(3, q, 2).wait_send()
        for c in next_sends(q):
            c.wait_send()

    @pl.when(odd)
    def _():
        for q in range(5):
            relay_send(q).wait_send()


def shards(interval_blocks, interval_pivots, boundary_pivots, interval_residuals):
    blocks, pivots, residuals = interval_blocks[0], interval_pivots[0], interval_residuals[0]
    nb, share = blocks.shape[1], residuals.shape[1]
    vmem = pl.BlockSpec(memory_space=pltpu.VMEM)
    reduced, rhs = pl.pallas_call(
        body,
        out_shape=(jax.ShapeDtypeStruct((nb, nb), BF), jax.ShapeDtypeStruct((1, share), F32)),
        in_specs=[pl.BlockSpec(memory_space=pl.ANY)] + [vmem] * 3,
        out_specs=(vmem, vmem),
        scratch_shapes=[
            pltpu.VMEM((STAGES, nb, 4 * nb), BF),
            pltpu.VMEM((STAGES, 4 * nb, nb), BF),
            pltpu.VMEM((STAGES, 16, 4 * nb), BF),
            pltpu.VMEM((2, 16, nb), BF),
            pltpu.VMEM((nb, nb), BF),
            pltpu.VMEM((16, nb), BF),
            pltpu.VMEM((nb, 4 * nb), BF),
            pltpu.VMEM((4 * nb, 4 * nb), BF),
            pltpu.VMEM((8, 4 * nb), jnp.int32),
            pltpu.VMEM((8, share), F32),
            pltpu.VMEM((8, nb), F32),
            pltpu.VMEM((16, nb), F32),
            pltpu.VMEM((16, nb), F32),
            pltpu.SemaphoreType.DMA((4,)),
            pltpu.SemaphoreType.DMA((3,)),
            pltpu.SemaphoreType.DMA((3,)),
            pltpu.SemaphoreType.DMA((HALVES, 3, 2)),
            pltpu.SemaphoreType.DMA((HALVES, 3, 2)),
            pltpu.SemaphoreType.DMA((STAGES, 4, 5)),
            pltpu.SemaphoreType.DMA((STAGES, 4, 5)),
            pltpu.SemaphoreType.DMA((5,)),
            pltpu.SemaphoreType.DMA((5,)),
            pltpu.SemaphoreType.DMA((STAGES, 2, 5)),
        ],
        compiler_params=pltpu.CompilerParams(
            collective_id=0, has_side_effects=True, vmem_limit_bytes=60 * 2**20
        ),
        name="newton",
    )(blocks, pivots, boundary_pivots, residuals)
    return reduced[None], rhs


def solution(mesh):
    placed = (
        P("loop", None, "row", "col"),
        P("loop", None, None),
        P(),
        P("loop", None, ("row", "col")),
    )
    return jax.shard_map(
        shards,
        mesh=mesh,
        in_specs=placed,
        out_specs=(P("loop", "row", "col"), P("loop", ("row", "col"))),
        check_vma=False,
    )
```

```python
import jax
import jax.numpy as jnp
from jax import lax
from jax.experimental import pallas as pl
from jax.experimental.pallas import tpu as pltpu
from jax.sharding import PartitionSpec as P

MESH = pl.DeviceIdType.MESH
BF, F32 = jnp.bfloat16, jnp.float32
NT = (((1,), (1,)), ((), ()))

FIRST, SECOND, PASSED = 0, 1, 2
STAGES, HALVES, VECTOR = 5, 10, 4


def body(w_ref, ipiv_ref, bpiv_ref, res_ref, out_ref, rhs_ref, gath, panel, vecs, own_vec, relay, relay_vec, perm, hot, pivs,
         gsend, gbuf, rbuf, held, load_sem, gs_sem, gr_sem, ys_sem, yr_sem, ps_sem, pr_sem, rs_sem, rr_sem, fs_sem):
    loop, row, col = lax.axis_index("loop"), lax.axis_index("row"), lax.axis_index("col")
    n_loop, n_row, n_col = lax.axis_size("loop"), lax.axis_size("row"), lax.axis_size("col")
    nb = perm.shape[0]
    half, quarter = nb // 2, nb // 4
    share = res_ref.shape[1]
    odd = lax.rem(loop, 2) == 1
    even = lax.rem(loop, 2) == 0
    own_lanes = pl.ds(0, nb)

    def at(dloop=0, row_=None, dcol=0):
        return {
            "loop": lax.rem(loop + dloop + n_loop, n_loop),
            "row": row if row_ is None else row_,
            "col": lax.rem(col + dcol + n_col, n_col),
        }

    sibling = row + 1 - 2 * lax.rem(row, 2)
    across = lax.rem(row + 2, n_row)

    def copy(src, dst, ssem, rsem, dev):
        return pltpu.make_async_remote_copy(
            src_ref=src, dst_ref=dst, send_sem=ssem, recv_sem=rsem, device_id=dev, device_id_type=MESH
        )

    def y_copy(j, k, direction):
        s, h = lax.div(j, 2), lax.rem(j, 2)
        near = 1 + direction
        offset = (direction + (k == SECOND)) % 2 * quarter
        rows = pl.ds(pl.multiple_of(h * half + offset, quarter), quarter)
        near_lanes = pl.ds(near * nb, nb)
        if k == PASSED:
            src, dst = gath.at[s, rows, near_lanes], gath.at[s, rows, pl.ds(3 * nb, nb)]
        else:
            src, dst = gath.at[s, rows, own_lanes], gath.at[s, rows, near_lanes]
        return copy(src, dst, ys_sem.at[j, k, direction], yr_sem.at[j, k, direction], at(dcol=1 - 2 * direction))

    def y_issue(j, k):
        for direction in (0, 1):
            y_copy(j, k, direction).start()

    def y_recv(j, k):
        for direction in (0, 1):
            y_copy(j, k, direction).wait_recv()

    def part(t, slot, q):
        if q == VECTOR:
            return vecs.at[t, :, pl.ds(slot * nb, nb)]
        return panel.at[t, pl.ds(slot * nb + q * quarter, quarter)]

    def own_part(t, q):
        if q == VECTOR:
            return own_vec.at[t - 3]
        return gath.at[t, pl.ds(q * quarter, quarter), own_lanes]

    def p_copy(t, q, src, slot, dev):
        return copy(src, part(t, slot, q), ps_sem.at[t, slot, q], pr_sem.at[t, slot, q], dev)

    def local_sends(t, q):
        return [p_copy(t, q, part(t, 0, q), 1, at(row_=sibling)), p_copy(t, q, part(t, 0, q), 2, at(row_=across))]

    def next_sends(q):
        src = own_part(3, q)
        return [p_copy(3, q, src, 0, at(dloop=1)), p_copy(3, q, src, 2, at(dloop=1, row_=across))]

    def relay_part(q):
        return relay_vec if q == VECTOR else relay.at[pl.ds(q * quarter, quarter)]

    def relay_send(q):
        return copy(own_part(3, q), relay_part(q), rs_sem.at[q], rr_sem.at[q], at(dloop=2))

    def relay_passes(q):
        src = relay_part(q)
        return [p_copy(3, q, src, 0, at(dloop=-1)), p_copy(3, q, src, 2, at(dloop=-1, row_=across))]

    def far_send(q):
        return p_copy(4, q, own_part(4, q), 0, at(dloop=2))

    def to_sibling(t, q, slot):
        return copy(part(t, slot, q), part(t, slot + 1, q), fs_sem.at[t, slot // 2, q], pr_sem.at[t, slot + 1, q], at(row_=sibling))

    def p_recv(t, slot, q):
        p_copy(t, q, part(t, slot, q), slot, at(row_=sibling)).wait_recv()

    def far_forward(t, q):
        p_recv(t, 2, q)
        to_sibling(t, q, 2).start()

    def join_part(t, q):
        p_recv(t, 1, q)
        p_recv(t, 3, q)

    def join(t):
        for q in range(5):
            join_part(t, q)

    def start_next(q):
        @pl.when(even)
        def _():
            for c in next_sends(q):
                c.start()

        @pl.when(odd)
        def _():
            relay_send(q).start()

    def pass_relay(q):
        @pl.when(odd)
        def _():
            relay_send(q).wait_recv()
            for c in relay_passes(q):
                c.start()

    def make_hot(s):
        for slot, dcol in enumerate((0, n_col - 1, 1, 2)):
            start = pl.multiple_of(lax.rem(col + dcol, n_col) * nb, nb)
            q = pivs[pl.ds(s, 1), pl.ds(start, nb)]

            def one(row_slot, carry):
                base = lax.rem(row + 2 * lax.div(row_slot, 2), n_row)
                base = base + (1 - 2 * lax.rem(base, 2)) * lax.rem(row_slot, 2)
                iota = lax.broadcasted_iota(jnp.int32, (nb, nb), 0)
                rows = pl.ds(pl.multiple_of(row_slot * nb, nb), nb)
                hot[rows, pl.ds(slot * nb, nb)] = jnp.where(iota == q - base * nb, 1.0, 0.0).astype(BF)
                return carry

            lax.fori_loop(0, 4, one, 0)

    def permute(j, lanes, first):
        s, h = lax.div(j, 2), lax.rem(j, 2)
        rows = pl.ds(pl.multiple_of(h * half, half), half)

        def one(part_, carry):
            targets = pl.ds(pl.multiple_of(part_ * 2 * nb, 2 * nb), 2 * nb)
            moved = lax.dot_general(gath[s, rows, lanes], hot[targets, lanes], NT, preferred_element_type=F32).astype(BF)
            if first:
                perm[rows, targets] = moved
            else:
                perm[rows, targets] += moved
            return carry

        lax.fori_loop(0, 2, one, 0)

    def product(s, h):
        rows = pl.ds(pl.multiple_of(h * half, half), half)
        value = jnp.dot(perm[rows, :], panel[s], preferred_element_type=F32).astype(BF)

        @pl.when(s == 0)
        def _():
            panel[2, rows, :] = value

        @pl.when((s >= 1) & (s < 4))
        def _():
            gath[s + 1, rows, own_lanes] = value

        @pl.when(s == 4)
        def _():
            out_ref[rows, :] = value

    def finish_vector(s):
        rbuf[...] = lax.dot_general(vecs[s], perm[...], NT, preferred_element_type=F32)

        @pl.when(s < 2)
        def _():
            rbuf[...] += gbuf[pl.ds(2 * s + 1, 1), :]

        @pl.when(s == 0)
        def _():
            vecs[2, :, own_lanes] = rbuf[...].astype(BF)

        @pl.when(s == 1)
        def _():
            held[...] = rbuf[...]

        @pl.when(s == 2)
        def _():
            rbuf[...] += held[...]

        @pl.when(s >= 3)
        def _():
            rbuf[...] += own_vec[s - 3].astype(F32)

        @pl.when((s >= 2) & (s < 4))
        def _():
            own_vec[s - 2] = rbuf[...].astype(BF)

    loads = []
    for s in range(2):
        loads.append(pltpu.make_async_copy(w_ref.at[2 * s + 1], gath.at[s, :, own_lanes], load_sem.at[2 * s]))
        loads.append(pltpu.make_async_copy(w_ref.at[2 * s], panel.at[s, pl.ds(0, nb)], load_sem.at[2 * s + 1]))
    for load in loads:
        load.start()
    barrier = pltpu.get_barrier_semaphore()
    partners = (
        at(dcol=1), at(dcol=-1), at(dcol=2), at(row_=sibling), at(row_=across),
        at(dloop=1), at(dloop=-1), at(dloop=1, row_=across), at(dloop=-1, row_=across), at(dloop=2), at(dloop=-2),
    )
    for partner in partners:
        pl.semaphore_signal(barrier, inc=1, device_id=partner, device_id_type=MESH)
    own_cols = pl.ds(pl.multiple_of(col * share, share), share)
    gsend[...] = jnp.zeros_like(gsend)
    gsend[pl.ds(0, 4), :] = res_ref[...].astype(F32)
    gbuf[:, own_cols] = gsend[...]
    for s, interval in enumerate((0, 2, 1)):
        pivs[pl.ds(s, 1), :] = ipiv_ref[pl.ds(interval, 1), :]
    pivs[pl.ds(3, 1), :] = bpiv_ref[pl.ds(loop, 1), :]
    pivs[pl.ds(4, 1), :] = bpiv_ref[pl.ds(lax.rem(loop + n_loop - 1, n_loop), 1), :]
    for load in loads:
        load.wait()
    pl.semaphore_wait(barrier, len(partners))

    def g_copy(i, dcol, holder):
        cols = pl.ds(pl.multiple_of(lax.rem(col + holder + n_col, n_col) * share, share), share)
        return copy(gsend, gbuf.at[:, cols], gs_sem.at[i], gr_sem.at[i], at(dcol=dcol))

    for j in (0, 1):
        y_issue(j, FIRST)
        y_issue(j, SECOND)
    for i, dcol in enumerate((1, -1, 2)):
        g_copy(i, dcol, 0).start()
    for q in range(4):
        for c in local_sends(0, q):
            c.start()
    make_hot(0)
    for i, dcol in enumerate((-1, 1, 2)):
        g_copy(i, dcol, dcol).wait_recv()
    for s in (0, 1):
        vecs[s, :, own_lanes] = jnp.broadcast_to(gbuf[pl.ds(2 * s, 1), :], (16, nb)).astype(BF)
    for c in local_sends(0, VECTOR):
        c.start()

    def drain(j, carry):
        for k in (FIRST, SECOND, PASSED):
            for direction in (0, 1):
                y_copy(j, k, direction).wait_send()
        return carry

    def drain_panel(t, carry):
        for q in range(5):
            for c in local_sends(t, q):
                c.wait_send()
            to_sibling(t, q, 2).wait_send()
        return carry

    def drain_next():
        for q in range(5):
            for slot in (0, 2):
                to_sibling(3, q, slot).wait_send()
            for c in next_sends(q):
                c.wait_send()

        @pl.when(odd)
        def _():
            for q in range(5):
                relay_send(q).wait_send()

    def step(j, carry):
        s, h = lax.div(j, 2), lax.rem(j, 2)

        def on(number, *actions):
            @pl.when(j == number)
            def _():
                for action, qs in actions:
                    for q in qs:
                        action(q)

        def first_far(q):
            far_forward(0, q)
            for c in local_sends(1, q):
                c.start()

        def second_far(q):
            far_forward(1, q)

        def third_far(q):
            far_forward(2, q)

        def pass_next(q):
            for slot in (0, 2):
                p_recv(3, slot, q)
                to_sibling(3, q, slot).start()

        def receive_far(q):
            p_recv(4, 0, q)
            for c in local_sends(4, q):
                c.start()

        def last_far(q):
            far_forward(4, q)

        @pl.when((j == 0) | (j == 6) | (j == 8))
        def _():
            y_recv(j, FIRST)
            y_issue(j, PASSED)

        on(6, (pass_relay, (1,)), (pass_next, (0,)))
        on(8, (receive_far, (0,)))

        @pl.when((h == 0) & (s > 0))
        def _():
            make_hot(s)

        on(8, (receive_far, (1,)))
        y_recv(j, SECOND)
        for last, new in ((0, 2), (1, 3)):
            @pl.when(j == last)
            def _():
                y_issue(new, FIRST)
                y_issue(new, SECOND)

        on(6, (pass_next, (1,)), (pass_relay, (2,)))
        on(7, (pass_next, (2,)))
        on(9, (last_far, (1, 2)))
        permute(j, pl.ds(0, 3 * nb), True)
        on(0, (first_far, (0, 1, 2, 3, VECTOR)))
        on(1, (second_far, (0, 1)))
        on(2, (second_far, (2, 3, VECTOR)))
        on(3, (third_far, (0, 1, 2, 3, VECTOR)))
        on(5, (pass_relay, (0,)))
        on(6, (pass_relay, (3, VECTOR)))
        on(7, (pass_next, (3, VECTOR)))
        on(8, (receive_far, (2,)))
        on(9, (last_far, (3, VECTOR)))
        @pl.when((j < 5) | (j == 6) | (j == 8))
        def _():
            y_recv(j + 1, FIRST)
            y_issue(j + 1, PASSED)

        y_recv(j, PASSED)
        permute(j, pl.ds(3 * nb, nb), False)
        on(8, (receive_far, (3, VECTOR)), (last_far, (0,)))

        @pl.when((h == 0) & (s < 3))
        def _():
            join(s)

        on(7, (join, (3,)))

        @pl.when(j == 9)
        def _():
            join_part(4, VECTOR)
            finish_vector(4)
            lax.fori_loop(0, HALVES - 1, drain, 0)
            lax.fori_loop(0, 3, drain_panel, 0)
            drain_next()
            for q in range(VECTOR):
                join_part(4, q)

        def multiply(hh, carry):
            product(s, hh)
            return carry

        low = jnp.where(s < 3, h, 0)
        high = jnp.where((s < 3) | (h == 1), h + 1, 0)
        lax.fori_loop(low, high, multiply, 0)

        for done, new in ((2, (4,)), (3, (5,)), (4, (6,)), (5, (7,)), (7, (8, 9))):
            @pl.when(j == done)
            def _():
                for n in new:
                    y_issue(n, FIRST)
                    y_issue(n, SECOND)

        def start_third(q):
            for c in local_sends(2, q):
                c.start()

        def start_far(q):
            far_send(q).start()

        on(0, (start_third, (0, 1)))
        on(1, (start_third, (2, 3)))
        on(4, (start_next, (0, 1)))
        on(5, (start_next, (2, 3)))
        on(7, (start_far, (0, 1, 2, 3)))

        @pl.when((h == 1) & (s < 4))
        def _():
            finish_vector(s)

        on(1, (start_third, (VECTOR,)))
        on(5, (start_next, (VECTOR,)))
        on(7, (start_far, (VECTOR,)))
        return carry

    lax.fori_loop(0, HALVES, step, 0)
    rhs_ref[...] = rbuf[pl.ds(0, 1), own_cols]

    for i, dcol in enumerate((1, -1, 2)):
        g_copy(i, dcol, 0).wait_send()
    drain(HALVES - 1, 0)
    drain_panel(4, 0)
    for q in range(5):
        far_send(q).wait_send()


def shards(interval_blocks, interval_pivots, boundary_pivots, interval_residuals):
    blocks, pivots, residuals = interval_blocks[0], interval_pivots[0], interval_residuals[0]
    nb, share = blocks.shape[1], residuals.shape[1]
    vmem = pl.BlockSpec(memory_space=pltpu.VMEM)
    reduced, rhs = pl.pallas_call(
        body,
        out_shape=(jax.ShapeDtypeStruct((nb, nb), BF), jax.ShapeDtypeStruct((1, share), F32)),
        in_specs=[pl.BlockSpec(memory_space=pl.ANY)] + [vmem] * 3,
        out_specs=(vmem, vmem),
        scratch_shapes=[
            pltpu.VMEM((STAGES, nb, 4 * nb), BF),
            pltpu.VMEM((STAGES, 4 * nb, nb), BF),
            pltpu.VMEM((STAGES, 16, 4 * nb), BF),
            pltpu.VMEM((2, 16, nb), BF),
            pltpu.VMEM((nb, nb), BF),
            pltpu.VMEM((16, nb), BF),
            pltpu.VMEM((nb, 4 * nb), BF),
            pltpu.VMEM((4 * nb, 4 * nb), BF),
            pltpu.VMEM((8, 4 * nb), jnp.int32),
            pltpu.VMEM((8, share), F32),
            pltpu.VMEM((8, nb), F32),
            pltpu.VMEM((16, nb), F32),
            pltpu.VMEM((16, nb), F32),
            pltpu.SemaphoreType.DMA((4,)),
            pltpu.SemaphoreType.DMA((3,)),
            pltpu.SemaphoreType.DMA((3,)),
            pltpu.SemaphoreType.DMA((HALVES, 3, 2)),
            pltpu.SemaphoreType.DMA((HALVES, 3, 2)),
            pltpu.SemaphoreType.DMA((STAGES, 4, 5)),
            pltpu.SemaphoreType.DMA((STAGES, 4, 5)),
            pltpu.SemaphoreType.DMA((5,)),
            pltpu.SemaphoreType.DMA((5,)),
            pltpu.SemaphoreType.DMA((STAGES, 2, 5)),
        ],
        compiler_params=pltpu.CompilerParams(
            collective_id=0, has_side_effects=True, vmem_limit_bytes=60 * 2**20
        ),
        name="newton",
    )(blocks, pivots, boundary_pivots, residuals)
    return reduced[None], rhs


def solution(mesh):
    placed = (
        P("loop", None, "row", "col"),
        P("loop", None, None),
        P(),
        P("loop", None, ("row", "col")),
    )
    return jax.shard_map(
        shards,
        mesh=mesh,
        in_specs=placed,
        out_specs=(P("loop", "row", "col"), P("loop", ("row", "col"))),
        check_vma=False,
    )
```

```python
import jax
import jax.numpy as jnp
from jax import lax
from jax.experimental import pallas as pl
from jax.experimental.pallas import tpu as pltpu
from jax.sharding import PartitionSpec as P

MESH = pl.DeviceIdType.MESH
BF, F32 = jnp.bfloat16, jnp.float32
NT = (((1,), (1,)), ((), ()))

FIRST, SECOND, PASSED = 0, 1, 2
STAGES, HALVES, VECTOR = 5, 10, 4


def body(w_ref, ipiv_ref, bpiv_ref, res_ref, out_ref, rhs_ref, gath, panel, vecs, own_vec, relay, relay_vec, perm, hot, pivs,
         gsend, gbuf, rbuf, held, load_sem, gs_sem, gr_sem, ys_sem, yr_sem, ps_sem, pr_sem, rs_sem, rr_sem, fs_sem):
    loop, row, col = lax.axis_index("loop"), lax.axis_index("row"), lax.axis_index("col")
    n_loop, n_row, n_col = lax.axis_size("loop"), lax.axis_size("row"), lax.axis_size("col")
    nb = perm.shape[0]
    half, quarter = nb // 2, nb // 4
    share = res_ref.shape[1]
    odd = lax.rem(loop, 2) == 1
    even = lax.rem(loop, 2) == 0
    own_lanes = pl.ds(0, nb)

    def at(dloop=0, row_=None, dcol=0):
        return {
            "loop": lax.rem(loop + dloop + n_loop, n_loop),
            "row": row if row_ is None else row_,
            "col": lax.rem(col + dcol + n_col, n_col),
        }

    sibling = row + 1 - 2 * lax.rem(row, 2)
    across = lax.rem(row + 2, n_row)

    def copy(src, dst, ssem, rsem, dev):
        return pltpu.make_async_remote_copy(
            src_ref=src, dst_ref=dst, send_sem=ssem, recv_sem=rsem, device_id=dev, device_id_type=MESH
        )

    def y_copy(j, k, direction):
        s, h = lax.div(j, 2), lax.rem(j, 2)
        near = 1 + direction
        offset = (direction + (k == SECOND)) % 2 * quarter
        rows = pl.ds(pl.multiple_of(h * half + offset, quarter), quarter)
        near_lanes = pl.ds(near * nb, nb)
        if k == PASSED:
            src, dst = gath.at[s, rows, near_lanes], gath.at[s, rows, pl.ds(3 * nb, nb)]
        else:
            src, dst = gath.at[s, rows, own_lanes], gath.at[s, rows, near_lanes]
        return copy(src, dst, ys_sem.at[j, k, direction], yr_sem.at[j, k, direction], at(dcol=1 - 2 * direction))

    def y_issue(j, k):
        for direction in (0, 1):
            y_copy(j, k, direction).start()

    def y_recv(j, k):
        for direction in (0, 1):
            y_copy(j, k, direction).wait_recv()

    def part(t, slot, q):
        if q == VECTOR:
            return vecs.at[t, :, pl.ds(slot * nb, nb)]
        return panel.at[t, pl.ds(slot * nb + q * quarter, quarter)]

    def own_part(t, q):
        if q == VECTOR:
            return own_vec.at[t - 3]
        return gath.at[t, pl.ds(q * quarter, quarter), own_lanes]

    def p_copy(t, q, src, slot, dev):
        return copy(src, part(t, slot, q), ps_sem.at[t, slot, q], pr_sem.at[t, slot, q], dev)

    def local_sends(t, q):
        return [p_copy(t, q, part(t, 0, q), 1, at(row_=sibling)), p_copy(t, q, part(t, 0, q), 2, at(row_=across))]

    def next_sends(q):
        src = own_part(3, q)
        return [p_copy(3, q, src, 0, at(dloop=1)), p_copy(3, q, src, 2, at(dloop=1, row_=across))]

    def relay_part(q):
        return relay_vec if q == VECTOR else relay.at[pl.ds(q * quarter, quarter)]

    def relay_send(q):
        return copy(own_part(3, q), relay_part(q), rs_sem.at[q], rr_sem.at[q], at(dloop=2))

    def relay_passes(q):
        src = relay_part(q)
        return [p_copy(3, q, src, 0, at(dloop=-1)), p_copy(3, q, src, 2, at(dloop=-1, row_=across))]

    def far_send(q):
        return p_copy(4, q, own_part(4, q), 0, at(dloop=2))

    def to_sibling(t, q, slot):
        return copy(part(t, slot, q), part(t, slot + 1, q), fs_sem.at[t, slot // 2, q], pr_sem.at[t, slot + 1, q], at(row_=sibling))

    def p_recv(t, slot, q):
        p_copy(t, q, part(t, slot, q), slot, at(row_=sibling)).wait_recv()

    def far_forward(t, q):
        p_recv(t, 2, q)
        to_sibling(t, q, 2).start()

    def join_part(t, q):
        p_recv(t, 1, q)
        p_recv(t, 3, q)

    def join(t):
        for q in range(5):
            join_part(t, q)

    def start_next(q):
        @pl.when(even)
        def _():
            for c in next_sends(q):
                c.start()

        @pl.when(odd)
        def _():
            relay_send(q).start()

    def pass_relay(q):
        @pl.when(odd)
        def _():
            relay_send(q).wait_recv()
            for c in relay_passes(q):
                c.start()

    def make_hot(s):
        for slot, dcol in enumerate((0, n_col - 1, 1, 2)):
            start = pl.multiple_of(lax.rem(col + dcol, n_col) * nb, nb)
            q = pivs[pl.ds(s, 1), pl.ds(start, nb)]

            def one(row_slot, carry):
                base = lax.rem(row + 2 * lax.div(row_slot, 2), n_row)
                base = base + (1 - 2 * lax.rem(base, 2)) * lax.rem(row_slot, 2)
                iota = lax.broadcasted_iota(jnp.int32, (nb, nb), 0)
                rows = pl.ds(pl.multiple_of(row_slot * nb, nb), nb)
                hot[rows, pl.ds(slot * nb, nb)] = jnp.where(iota == q - base * nb, 1.0, 0.0).astype(BF)
                return carry

            lax.fori_loop(0, 4, one, 0)

    def permute(j, lanes, first):
        s, h = lax.div(j, 2), lax.rem(j, 2)
        rows = pl.ds(pl.multiple_of(h * half, half), half)

        def one(part_, carry):
            targets = pl.ds(pl.multiple_of(part_ * 2 * nb, 2 * nb), 2 * nb)
            moved = lax.dot_general(gath[s, rows, lanes], hot[targets, lanes], NT, preferred_element_type=F32).astype(BF)
            if first:
                perm[rows, targets] = moved
            else:
                perm[rows, targets] += moved
            return carry

        lax.fori_loop(0, 2, one, 0)

    def product(s, h):
        rows = pl.ds(pl.multiple_of(h * half, half), half)
        value = jnp.dot(perm[rows, :], panel[s], preferred_element_type=F32).astype(BF)

        @pl.when(s == 0)
        def _():
            panel[2, rows, :] = value

        @pl.when((s >= 1) & (s < 4))
        def _():
            gath[s + 1, rows, own_lanes] = value

        @pl.when(s == 4)
        def _():
            out_ref[rows, :] = value

    def finish_vector(s):
        rbuf[...] = lax.dot_general(vecs[s], perm[...], NT, preferred_element_type=F32)

        @pl.when(s < 2)
        def _():
            rbuf[...] += gbuf[pl.ds(2 * s + 1, 1), :]

        @pl.when(s == 0)
        def _():
            vecs[2, :, own_lanes] = rbuf[...].astype(BF)

        @pl.when(s == 1)
        def _():
            held[...] = rbuf[...]

        @pl.when(s == 2)
        def _():
            rbuf[...] += held[...]

        @pl.when(s >= 3)
        def _():
            rbuf[...] += own_vec[s - 3].astype(F32)

        @pl.when((s >= 2) & (s < 4))
        def _():
            own_vec[s - 2] = rbuf[...].astype(BF)

    loads = []
    for s in range(2):
        loads.append(pltpu.make_async_copy(w_ref.at[2 * s + 1], gath.at[s, :, own_lanes], load_sem.at[2 * s]))
        loads.append(pltpu.make_async_copy(w_ref.at[2 * s], panel.at[s, pl.ds(0, nb)], load_sem.at[2 * s + 1]))
    for load in loads:
        load.start()
    barrier = pltpu.get_barrier_semaphore()
    partners = (
        at(dcol=1), at(dcol=-1), at(dcol=2), at(row_=sibling), at(row_=across),
        at(dloop=1), at(dloop=-1), at(dloop=1, row_=across), at(dloop=-1, row_=across), at(dloop=2), at(dloop=-2),
    )
    for partner in partners:
        pl.semaphore_signal(barrier, inc=1, device_id=partner, device_id_type=MESH)
    own_cols = pl.ds(pl.multiple_of(col * share, share), share)
    gsend[...] = jnp.zeros_like(gsend)
    gsend[pl.ds(0, 4), :] = res_ref[...].astype(F32)
    gbuf[:, own_cols] = gsend[...]
    for s, interval in enumerate((0, 2, 1)):
        pivs[pl.ds(s, 1), :] = ipiv_ref[0, pl.ds(interval, 1), :]
    pivs[pl.ds(3, 1), :] = bpiv_ref[pl.ds(loop, 1), :]
    pivs[pl.ds(4, 1), :] = bpiv_ref[pl.ds(lax.rem(loop + n_loop - 1, n_loop), 1), :]
    for load in loads:
        load.wait()
    pl.semaphore_wait(barrier, len(partners))

    def g_copy(i, dcol, holder):
        cols = pl.ds(pl.multiple_of(lax.rem(col + holder + n_col, n_col) * share, share), share)
        return copy(gsend, gbuf.at[:, cols], gs_sem.at[i], gr_sem.at[i], at(dcol=dcol))

    for j in (0, 1):
        y_issue(j, FIRST)
        y_issue(j, SECOND)
    for i, dcol in enumerate((1, -1, 2)):
        g_copy(i, dcol, 0).start()
    for q in range(4):
        for c in local_sends(0, q):
            c.start()
    make_hot(0)
    for i, dcol in enumerate((-1, 1, 2)):
        g_copy(i, dcol, dcol).wait_recv()
    for s in (0, 1):
        vecs[s, :, own_lanes] = jnp.broadcast_to(gbuf[pl.ds(2 * s, 1), :], (16, nb)).astype(BF)
    for c in local_sends(0, VECTOR):
        c.start()

    def drain(j, carry):
        for k in (FIRST, SECOND, PASSED):
            for direction in (0, 1):
                y_copy(j, k, direction).wait_send()
        return carry

    def drain_panel(t, carry):
        for q in range(5):
            for c in local_sends(t, q):
                c.wait_send()
            to_sibling(t, q, 2).wait_send()
        return carry

    def drain_next():
        for q in range(5):
            for slot in (0, 2):
                to_sibling(3, q, slot).wait_send()
            for c in next_sends(q):
                c.wait_send()

        @pl.when(odd)
        def _():
            for q in range(5):
                relay_send(q).wait_send()

    def step(j, carry):
        s, h = lax.div(j, 2), lax.rem(j, 2)

        def on(number, *actions):
            @pl.when(j == number)
            def _():
                for action, qs in actions:
                    for q in qs:
                        action(q)

        def first_far(q):
            far_forward(0, q)
            for c in local_sends(1, q):
                c.start()

        def second_far(q):
            far_forward(1, q)

        def third_far(q):
            far_forward(2, q)

        def pass_next(q):
            for slot in (0, 2):
                p_recv(3, slot, q)
                to_sibling(3, q, slot).start()

        def receive_far(q):
            p_recv(4, 0, q)
            for c in local_sends(4, q):
                c.start()

        def last_far(q):
            far_forward(4, q)

        @pl.when((j == 0) | (j == 6) | (j == 8))
        def _():
            y_recv(j, FIRST)
            y_issue(j, PASSED)

        on(6, (pass_relay, (1,)), (pass_next, (0,)))
        on(8, (receive_far, (0,)))

        @pl.when((j == 2) | (j == 4) | (j == 6))
        def _():
            make_hot(s)

        permute(j, own_lanes, True)
        on(8, (receive_far, (1,)))
        y_recv(j, SECOND)
        for last, new in ((0, 2), (1, 3)):
            @pl.when(j == last)
            def _():
                y_issue(new, FIRST)
                y_issue(new, SECOND)

        on(6, (pass_next, (1,)), (pass_relay, (2,)))
        on(7, (pass_next, (2,)))
        on(8, (receive_far, (2,)))
        on(9, (last_far, (2,)))

        @pl.when(j == 8)
        def _():
            y_recv(9, FIRST)
            y_issue(9, PASSED)

        permute(j, pl.ds(nb, 2 * nb), False)
        on(0, (first_far, (0, 1, 2, 3, VECTOR)))
        on(1, (second_far, (0, 1)))
        on(2, (second_far, (2, 3, VECTOR)))
        on(3, (third_far, (0, 1, 2, 3, VECTOR)))
        on(5, (pass_relay, (0,)))
        on(6, (pass_relay, (3, VECTOR)))
        on(7, (pass_next, (3, VECTOR)))
        on(8, (receive_far, (3, VECTOR)), (last_far, (0,)))
        on(9, (last_far, (3, VECTOR)))
        @pl.when((j < 5) | (j == 6))
        def _():
            y_recv(j + 1, FIRST)
            y_issue(j + 1, PASSED)

        y_recv(j, PASSED)
        permute(j, pl.ds(3 * nb, nb), False)
        on(8, (last_far, (1,)))

        @pl.when((h == 0) & (s < 3))
        def _():
            join(s)

        @pl.when(j == 7)
        def _():
            make_hot(4)

        on(7, (join, (3,)))

        @pl.when(j == 9)
        def _():
            join_part(4, VECTOR)
            finish_vector(4)
            lax.fori_loop(0, HALVES - 1, drain, 0)
            lax.fori_loop(0, 3, drain_panel, 0)
            drain_next()
            for q in range(VECTOR):
                join_part(4, q)

        def multiply(hh, carry):
            product(s, hh)
            return carry

        low = jnp.where(s < 3, h, 0)
        high = jnp.where((s < 3) | (h == 1), h + 1, 0)
        lax.fori_loop(low, high, multiply, 0)

        for done, new in ((2, (4,)), (3, (5,)), (4, (6,)), (5, (7,)), (7, (8, 9))):
            @pl.when(j == done)
            def _():
                for n in new:
                    y_issue(n, FIRST)
                    y_issue(n, SECOND)

        def start_third(q):
            for c in local_sends(2, q):
                c.start()

        def start_far(q):
            far_send(q).start()

        on(0, (start_third, (0, 1)))
        on(1, (start_third, (2, 3)))
        on(4, (start_next, (0, 1)))
        on(5, (start_next, (2, 3)))
        on(7, (start_far, (0, 1, 2, 3)))

        @pl.when((h == 1) & (s < 4))
        def _():
            finish_vector(s)

        on(1, (start_third, (VECTOR,)))
        on(5, (start_next, (VECTOR,)))
        on(7, (start_far, (VECTOR,)))
        return carry

    lax.fori_loop(0, HALVES, step, 0)
    rhs_ref[...] = rbuf[pl.ds(0, 1), own_cols]

    for i, dcol in enumerate((1, -1, 2)):
        g_copy(i, dcol, 0).wait_send()
    drain(HALVES - 1, 0)
    drain_panel(4, 0)
    for q in range(5):
        far_send(q).wait_send()


def shards(interval_blocks, interval_pivots, boundary_pivots, interval_residuals):
    blocks, residuals = interval_blocks[0], interval_residuals[0]
    nb, share = blocks.shape[1], residuals.shape[1]
    vmem = pl.BlockSpec(memory_space=pltpu.VMEM)
    reduced, rhs = pl.pallas_call(
        body,
        out_shape=(jax.ShapeDtypeStruct((nb, nb), BF), jax.ShapeDtypeStruct((1, share), F32)),
        in_specs=[pl.BlockSpec(memory_space=pl.ANY)] + [vmem] * 3,
        out_specs=(vmem, vmem),
        scratch_shapes=[
            pltpu.VMEM((STAGES, nb, 4 * nb), BF),
            pltpu.VMEM((STAGES, 4 * nb, nb), BF),
            pltpu.VMEM((STAGES, 16, 4 * nb), BF),
            pltpu.VMEM((2, 16, nb), BF),
            pltpu.VMEM((nb, nb), BF),
            pltpu.VMEM((16, nb), BF),
            pltpu.VMEM((nb, 4 * nb), BF),
            pltpu.VMEM((4 * nb, 4 * nb), BF),
            pltpu.VMEM((8, 4 * nb), jnp.int32),
            pltpu.VMEM((8, share), F32),
            pltpu.VMEM((8, nb), F32),
            pltpu.VMEM((16, nb), F32),
            pltpu.VMEM((16, nb), F32),
            pltpu.SemaphoreType.DMA((4,)),
            pltpu.SemaphoreType.DMA((3,)),
            pltpu.SemaphoreType.DMA((3,)),
            pltpu.SemaphoreType.DMA((HALVES, 3, 2)),
            pltpu.SemaphoreType.DMA((HALVES, 3, 2)),
            pltpu.SemaphoreType.DMA((STAGES, 4, 5)),
            pltpu.SemaphoreType.DMA((STAGES, 4, 5)),
            pltpu.SemaphoreType.DMA((5,)),
            pltpu.SemaphoreType.DMA((5,)),
            pltpu.SemaphoreType.DMA((STAGES, 2, 5)),
        ],
        compiler_params=pltpu.CompilerParams(
            collective_id=0, has_side_effects=True, vmem_limit_bytes=60 * 2**20
        ),
        name="newton",
    )(blocks, interval_pivots, boundary_pivots, residuals)
    return reduced[None], rhs


def solution(mesh):
    placed = (
        P("loop", None, "row", "col"),
        P("loop", None, None),
        P(),
        P("loop", None, ("row", "col")),
    )
    return jax.shard_map(
        shards,
        mesh=mesh,
        in_specs=placed,
        out_specs=(P("loop", "row", "col"), P("loop", ("row", "col"))),
        check_vma=False,
    )
```

```python
import jax
import jax.numpy as jnp
from jax import lax
from jax.experimental import pallas as pl
from jax.experimental.pallas import tpu as pltpu
from jax.sharding import PartitionSpec as P

MESH = pl.DeviceIdType.MESH
BF, F32 = jnp.bfloat16, jnp.float32
NT = (((1,), (1,)), ((), ()))

FIRST, SECOND, PASSED = 0, 1, 2
STAGES, HALVES, VECTOR = 5, 10, 4


def body(w_ref, ipiv_ref, bpiv_ref, res_ref, out_ref, rhs_ref, gath, panel, vecs, own_vec, relay, relay_vec, perm, hot, pivs,
         gsend, gbuf, rbuf, held, load_sem, gs_sem, gr_sem, ys_sem, yr_sem, ps_sem, pr_sem, rs_sem, rr_sem, fs_sem):
    loop, row, col = lax.axis_index("loop"), lax.axis_index("row"), lax.axis_index("col")
    n_loop, n_row, n_col = lax.axis_size("loop"), lax.axis_size("row"), lax.axis_size("col")
    nb = perm.shape[0]
    half, quarter = nb // 2, nb // 4
    share = res_ref.shape[1]
    odd = lax.rem(loop, 2) == 1
    even = lax.rem(loop, 2) == 0
    own_lanes = pl.ds(0, nb)

    def at(dloop=0, row_=None, dcol=0):
        return {
            "loop": lax.rem(loop + dloop + n_loop, n_loop),
            "row": row if row_ is None else row_,
            "col": lax.rem(col + dcol + n_col, n_col),
        }

    sibling = row + 1 - 2 * lax.rem(row, 2)
    across = lax.rem(row + 2, n_row)

    def copy(src, dst, ssem, rsem, dev):
        return pltpu.make_async_remote_copy(
            src_ref=src, dst_ref=dst, send_sem=ssem, recv_sem=rsem, device_id=dev, device_id_type=MESH
        )

    def y_copy(j, k, direction):
        s, h = lax.div(j, 2), lax.rem(j, 2)
        near = 1 + direction
        offset = (direction + (k == SECOND)) % 2 * quarter
        rows = pl.ds(pl.multiple_of(h * half + offset, quarter), quarter)
        near_lanes = pl.ds(near * nb, nb)
        if k == PASSED:
            src, dst = gath.at[s, rows, near_lanes], gath.at[s, rows, pl.ds(3 * nb, nb)]
        else:
            src, dst = gath.at[s, rows, own_lanes], gath.at[s, rows, near_lanes]
        return copy(src, dst, ys_sem.at[j, k, direction], yr_sem.at[j, k, direction], at(dcol=1 - 2 * direction))

    def y_issue(j, k):
        for direction in (0, 1):
            y_copy(j, k, direction).start()

    def y_recv(j, k):
        for direction in (0, 1):
            y_copy(j, k, direction).wait_recv()

    def part(t, slot, q):
        if q == VECTOR:
            return vecs.at[t, :, pl.ds(slot * nb, nb)]
        return panel.at[t, pl.ds(slot * nb + q * quarter, quarter)]

    def own_part(t, q):
        if q == VECTOR:
            return own_vec.at[t - 3]
        return gath.at[t, pl.ds(q * quarter, quarter), own_lanes]

    def p_copy(t, q, src, slot, dev):
        return copy(src, part(t, slot, q), ps_sem.at[t, slot, q], pr_sem.at[t, slot, q], dev)

    def local_sends(t, q):
        return [p_copy(t, q, part(t, 0, q), 1, at(row_=sibling)), p_copy(t, q, part(t, 0, q), 2, at(row_=across))]

    def next_sends(q):
        src = own_part(3, q)
        return [p_copy(3, q, src, 0, at(dloop=1)), p_copy(3, q, src, 2, at(dloop=1, row_=across))]

    def relay_part(q):
        return relay_vec if q == VECTOR else relay.at[pl.ds(q * quarter, quarter)]

    def relay_send(q):
        return copy(own_part(3, q), relay_part(q), rs_sem.at[q], rr_sem.at[q], at(dloop=2))

    def relay_passes(q):
        src = relay_part(q)
        return [p_copy(3, q, src, 0, at(dloop=-1)), p_copy(3, q, src, 2, at(dloop=-1, row_=across))]

    def far_send(q):
        return p_copy(4, q, own_part(4, q), 0, at(dloop=2))

    def to_sibling(t, q, slot):
        return copy(part(t, slot, q), part(t, slot + 1, q), fs_sem.at[t, slot // 2, q], pr_sem.at[t, slot + 1, q], at(row_=sibling))

    def p_recv(t, slot, q):
        p_copy(t, q, part(t, slot, q), slot, at(row_=sibling)).wait_recv()

    def far_forward(t, q):
        p_recv(t, 2, q)
        to_sibling(t, q, 2).start()

    def join_part(t, q):
        p_recv(t, 1, q)
        p_recv(t, 3, q)

    def join(t):
        for q in range(5):
            join_part(t, q)

    def start_next(q):
        @pl.when(even)
        def _():
            for c in next_sends(q):
                c.start()

        @pl.when(odd)
        def _():
            relay_send(q).start()

    def pass_relay(q):
        @pl.when(odd)
        def _():
            relay_send(q).wait_recv()
            for c in relay_passes(q):
                c.start()

    def make_hot(s):
        for slot, dcol in enumerate((0, n_col - 1, 1, 2)):
            start = pl.multiple_of(lax.rem(col + dcol, n_col) * nb, nb)
            q = pivs[pl.ds(s, 1), pl.ds(start, nb)]

            def one(row_slot, carry):
                base = lax.rem(row + 2 * lax.div(row_slot, 2), n_row)
                base = base + (1 - 2 * lax.rem(base, 2)) * lax.rem(row_slot, 2)
                iota = lax.broadcasted_iota(jnp.int16, (nb, nb), 0)
                wanted = jnp.broadcast_to((q - base * nb).astype(jnp.int16), (nb, nb))
                rows = pl.ds(pl.multiple_of(row_slot * nb, nb), nb)
                hot[rows, pl.ds(slot * nb, nb)] = jnp.where(iota == wanted, BF(1), BF(0))
                return carry

            lax.fori_loop(0, 4, one, 0)

    def permute(j, lanes, first):
        s, h = lax.div(j, 2), lax.rem(j, 2)
        rows = pl.ds(pl.multiple_of(h * half, half), half)

        def one(part_, carry):
            targets = pl.ds(pl.multiple_of(part_ * 2 * nb, 2 * nb), 2 * nb)
            moved = lax.dot_general(gath[s, rows, lanes], hot[targets, lanes], NT, preferred_element_type=F32).astype(BF)
            if first:
                perm[rows, targets] = moved
            else:
                perm[rows, targets] += moved
            return carry

        lax.fori_loop(0, 2, one, 0)

    def product(s, h):
        rows = pl.ds(pl.multiple_of(h * half, half), half)
        value = jnp.dot(perm[rows, :], panel[s], preferred_element_type=F32).astype(BF)

        @pl.when(s == 0)
        def _():
            panel[2, rows, :] = value

        @pl.when((s >= 1) & (s < 4))
        def _():
            gath[s + 1, rows, own_lanes] = value

        @pl.when(s == 4)
        def _():
            out_ref[rows, :] = value

    def finish_vector(s):
        rbuf[...] = lax.dot_general(vecs[s], perm[...], NT, preferred_element_type=F32)

        @pl.when(s < 2)
        def _():
            rbuf[...] += gbuf[pl.ds(2 * s + 1, 1), :]

        @pl.when(s == 0)
        def _():
            vecs[2, :, own_lanes] = rbuf[...].astype(BF)

        @pl.when(s == 1)
        def _():
            held[...] = rbuf[...]

        @pl.when(s == 2)
        def _():
            rbuf[...] += held[...]

        @pl.when(s >= 3)
        def _():
            rbuf[...] += own_vec[s - 3].astype(F32)

        @pl.when((s >= 2) & (s < 4))
        def _():
            own_vec[s - 2] = rbuf[...].astype(BF)

    loads = []
    for s in range(2):
        loads.append(pltpu.make_async_copy(w_ref.at[2 * s + 1], gath.at[s, :, own_lanes], load_sem.at[2 * s]))
        loads.append(pltpu.make_async_copy(w_ref.at[2 * s], panel.at[s, pl.ds(0, nb)], load_sem.at[2 * s + 1]))
    for load in loads:
        load.start()
    barrier = pltpu.get_barrier_semaphore()
    partners = (
        at(dcol=1), at(dcol=-1), at(dcol=2), at(row_=sibling), at(row_=across),
        at(dloop=1), at(dloop=-1), at(dloop=1, row_=across), at(dloop=-1, row_=across), at(dloop=2), at(dloop=-2),
    )
    for partner in partners:
        pl.semaphore_signal(barrier, inc=1, device_id=partner, device_id_type=MESH)
    own_cols = pl.ds(pl.multiple_of(col * share, share), share)
    gsend[...] = jnp.zeros_like(gsend)
    gsend[pl.ds(0, 4), :] = res_ref[...].astype(F32)
    gbuf[:, own_cols] = gsend[...]
    for s, interval in enumerate((0, 2, 1)):
        pivs[pl.ds(s, 1), :] = ipiv_ref[interval]
    pivs[pl.ds(3, 1), :] = bpiv_ref[pl.ds(loop, 1), :]
    pivs[pl.ds(4, 1), :] = bpiv_ref[pl.ds(lax.rem(loop + n_loop - 1, n_loop), 1), :]
    for load in loads:
        load.wait()
    pl.semaphore_wait(barrier, len(partners))

    def g_copy(i, dcol, holder):
        cols = pl.ds(pl.multiple_of(lax.rem(col + holder + n_col, n_col) * share, share), share)
        return copy(gsend, gbuf.at[:, cols], gs_sem.at[i], gr_sem.at[i], at(dcol=dcol))

    for j in (0, 1):
        y_issue(j, FIRST)
        y_issue(j, SECOND)
    for i, dcol in enumerate((1, -1, 2)):
        g_copy(i, dcol, 0).start()
    for q in range(4):
        for c in local_sends(0, q):
            c.start()
    make_hot(0)
    for i, dcol in enumerate((-1, 1, 2)):
        g_copy(i, dcol, dcol).wait_recv()
    for s in (0, 1):
        vecs[s, :, own_lanes] = jnp.broadcast_to(gbuf[pl.ds(2 * s, 1), :], (16, nb)).astype(BF)
    for c in local_sends(0, VECTOR):
        c.start()

    def drain(j, carry):
        for k in (FIRST, SECOND, PASSED):
            for direction in (0, 1):
                y_copy(j, k, direction).wait_send()
        return carry

    def drain_panel(t, carry):
        for q in range(5):
            for c in local_sends(t, q):
                c.wait_send()
            to_sibling(t, q, 2).wait_send()
        return carry

    def drain_next():
        for q in range(5):
            for slot in (0, 2):
                to_sibling(3, q, slot).wait_send()
            for c in next_sends(q):
                c.wait_send()

        @pl.when(odd)
        def _():
            for q in range(5):
                relay_send(q).wait_send()

    def step(j, carry):
        s, h = lax.div(j, 2), lax.rem(j, 2)

        def on(number, *actions):
            @pl.when(j == number)
            def _():
                for action, qs in actions:
                    for q in qs:
                        action(q)

        def first_far(q):
            far_forward(0, q)
            for c in local_sends(1, q):
                c.start()

        def second_far(q):
            far_forward(1, q)

        def third_far(q):
            far_forward(2, q)

        def pass_next(q):
            for slot in (0, 2):
                p_recv(3, slot, q)
                to_sibling(3, q, slot).start()

        def receive_far(q):
            p_recv(4, 0, q)
            for c in local_sends(4, q):
                c.start()

        def last_far(q):
            far_forward(4, q)

        @pl.when((j == 0) | (j == 6) | (j == 8))
        def _():
            y_recv(j, FIRST)
            y_issue(j, PASSED)

        on(6, (pass_relay, (1,)), (pass_next, (0,)))
        on(8, (receive_far, (0,)))

        @pl.when((j == 2) | (j == 4) | (j == 6))
        def _():
            make_hot(s)

        permute(j, own_lanes, True)
        on(8, (receive_far, (1,)))
        y_recv(j, SECOND)
        for last, new in ((0, 2), (1, 3)):
            @pl.when(j == last)
            def _():
                y_issue(new, FIRST)
                y_issue(new, SECOND)

        on(6, (pass_next, (1,)), (pass_relay, (2,)))
        on(7, (pass_next, (2,)))
        on(8, (receive_far, (2,)))
        on(9, (last_far, (2,)))

        @pl.when(j == 8)
        def _():
            y_recv(9, FIRST)
            y_issue(9, PASSED)

        permute(j, pl.ds(nb, 2 * nb), False)
        on(0, (first_far, (0, 1, 2, 3, VECTOR)))
        on(1, (second_far, (0, 1)))
        on(2, (second_far, (2, 3, VECTOR)))
        on(3, (third_far, (0, 1, 2, 3, VECTOR)))
        on(5, (pass_relay, (0,)))
        on(6, (pass_relay, (3, VECTOR)))
        on(7, (pass_next, (3, VECTOR)))
        on(8, (receive_far, (3, VECTOR)), (last_far, (0,)))
        on(9, (last_far, (3, VECTOR)))
        @pl.when((j < 5) | (j == 6))
        def _():
            y_recv(j + 1, FIRST)
            y_issue(j + 1, PASSED)

        y_recv(j, PASSED)
        permute(j, pl.ds(3 * nb, nb), False)
        on(8, (last_far, (1,)))

        @pl.when((h == 0) & (s < 3))
        def _():
            join(s)


        on(7, (join, (3,)))

        @pl.when(j == 9)
        def _():
            join_part(4, VECTOR)
            finish_vector(4)
            lax.fori_loop(0, HALVES - 1, drain, 0)
            lax.fori_loop(0, 3, drain_panel, 0)
            drain_next()
            for q in range(VECTOR):
                join_part(4, q)

        def multiply(hh, carry):
            product(s, hh)
            return carry

        low = jnp.where(s < 3, h, 0)
        high = jnp.where((s < 3) | (h == 1), h + 1, 0)
        lax.fori_loop(low, high, multiply, 0)

        for done, new in ((2, (4,)), (3, (5,)), (4, (6,)), (5, (7,)), (7, (8, 9))):
            @pl.when(j == done)
            def _():
                for n in new:
                    y_issue(n, FIRST)
                    y_issue(n, SECOND)

        def start_third(q):
            for c in local_sends(2, q):
                c.start()

        def start_far(q):
            far_send(q).start()

        on(0, (start_third, (0, 1)))
        on(1, (start_third, (2, 3)))
        on(4, (start_next, (0, 1)))
        on(5, (start_next, (2, 3)))
        on(7, (start_far, (0, 1, 2, 3)))

        @pl.when((h == 1) & (s < 4))
        def _():
            finish_vector(s)

        on(1, (start_third, (VECTOR,)))
        on(5, (start_next, (VECTOR,)))
        on(7, (start_far, (VECTOR,)), (make_hot, (4,)))
        return carry

    lax.fori_loop(0, HALVES, step, 0)
    rhs_ref[...] = rbuf[pl.ds(0, 1), own_cols]

    for i, dcol in enumerate((1, -1, 2)):
        g_copy(i, dcol, 0).wait_send()
    drain(HALVES - 1, 0)
    drain_panel(4, 0)
    for q in range(5):
        far_send(q).wait_send()


def shards(interval_blocks, interval_pivots, boundary_pivots, interval_residuals):
    blocks, residuals = interval_blocks[0], interval_residuals[0]
    nb, share = blocks.shape[1], residuals.shape[1]
    vmem = pl.BlockSpec(memory_space=pltpu.VMEM)
    reduced, rhs = pl.pallas_call(
        body,
        out_shape=(jax.ShapeDtypeStruct((nb, nb), BF), jax.ShapeDtypeStruct((1, share), F32)),
        in_specs=[pl.BlockSpec(memory_space=pl.ANY)] + [vmem] * 3,
        out_specs=(vmem, vmem),
        scratch_shapes=[
            pltpu.VMEM((STAGES, nb, 4 * nb), BF),
            pltpu.VMEM((STAGES, 4 * nb, nb), BF),
            pltpu.VMEM((STAGES, 16, 4 * nb), BF),
            pltpu.VMEM((2, 16, nb), BF),
            pltpu.VMEM((nb, nb), BF),
            pltpu.VMEM((16, nb), BF),
            pltpu.VMEM((nb, 4 * nb), BF),
            pltpu.VMEM((4 * nb, 4 * nb), BF),
            pltpu.VMEM((8, 4 * nb), jnp.int32),
            pltpu.VMEM((8, share), F32),
            pltpu.VMEM((8, nb), F32),
            pltpu.VMEM((16, nb), F32),
            pltpu.VMEM((16, nb), F32),
            pltpu.SemaphoreType.DMA((4,)),
            pltpu.SemaphoreType.DMA((3,)),
            pltpu.SemaphoreType.DMA((3,)),
            pltpu.SemaphoreType.DMA((HALVES, 3, 2)),
            pltpu.SemaphoreType.DMA((HALVES, 3, 2)),
            pltpu.SemaphoreType.DMA((STAGES, 4, 5)),
            pltpu.SemaphoreType.DMA((STAGES, 4, 5)),
            pltpu.SemaphoreType.DMA((5,)),
            pltpu.SemaphoreType.DMA((5,)),
            pltpu.SemaphoreType.DMA((STAGES, 2, 5)),
        ],
        compiler_params=pltpu.CompilerParams(
            collective_id=0, has_side_effects=True, vmem_limit_bytes=60 * 2**20
        ),
        name="newton",
    )(blocks, jnp.transpose(interval_pivots, (1, 0, 2)), boundary_pivots, residuals)
    return reduced[None], rhs


def solution(mesh):
    placed = (
        P("loop", None, "row", "col"),
        P("loop", None, None),
        P(),
        P("loop", None, ("row", "col")),
    )
    return jax.shard_map(
        shards,
        mesh=mesh,
        in_specs=placed,
        out_specs=(P("loop", "row", "col"), P("loop", ("row", "col"))),
        check_vma=False,
    )
```

```python
import jax
import jax.numpy as jnp
from jax import lax
from jax.experimental import pallas as pl
from jax.experimental.pallas import tpu as pltpu
from jax.sharding import PartitionSpec as P

MESH = pl.DeviceIdType.MESH
BF, F32 = jnp.bfloat16, jnp.float32
NT = (((1,), (1,)), ((), ()))

FIRST, SECOND, PASSED = 0, 1, 2
STAGES, HALVES, VECTOR = 5, 10, 4
RELAYED = (0, 2)


def body(w_ref, ipiv_ref, bpiv_ref, res_ref, out_ref, rhs_ref, gath, panel, vecs, own_vec, relay, perm, hot, pivs,
         gsend, gbuf, rbuf, held, load_sem, gs_sem, gr_sem, ys_sem, yr_sem, ps_sem, pr_sem, rs_sem, rr_sem, fs_sem):
    loop, row, col = lax.axis_index("loop"), lax.axis_index("row"), lax.axis_index("col")
    n_loop, n_row, n_col = lax.axis_size("loop"), lax.axis_size("row"), lax.axis_size("col")
    nb = perm.shape[0]
    half, quarter = nb // 2, nb // 4
    share = res_ref.shape[1]
    odd = lax.rem(loop, 2) == 1
    even = lax.rem(loop, 2) == 0
    own_lanes = pl.ds(0, nb)

    def at(dloop=0, row_=None, dcol=0):
        return {
            "loop": lax.rem(loop + dloop + n_loop, n_loop),
            "row": row if row_ is None else row_,
            "col": lax.rem(col + dcol + n_col, n_col),
        }

    sibling = row + 1 - 2 * lax.rem(row, 2)
    across = lax.rem(row + 2, n_row)

    def copy(src, dst, ssem, rsem, dev):
        return pltpu.make_async_remote_copy(
            src_ref=src, dst_ref=dst, send_sem=ssem, recv_sem=rsem, device_id=dev, device_id_type=MESH
        )

    def y_copy(j, k, direction):
        s, h = lax.div(j, 2), lax.rem(j, 2)
        near = 1 + direction
        offset = (direction + (k == SECOND)) % 2 * quarter
        rows = pl.ds(pl.multiple_of(h * half + offset, quarter), quarter)
        near_lanes = pl.ds(near * nb, nb)
        if k == PASSED:
            src, dst = gath.at[s, rows, near_lanes], gath.at[s, rows, pl.ds(3 * nb, nb)]
        else:
            src, dst = gath.at[s, rows, own_lanes], gath.at[s, rows, near_lanes]
        return copy(src, dst, ys_sem.at[j, k, direction], yr_sem.at[j, k, direction], at(dcol=1 - 2 * direction))

    def y_issue(j, k):
        for direction in (0, 1):
            y_copy(j, k, direction).start()

    def y_recv(j, k):
        for direction in (0, 1):
            y_copy(j, k, direction).wait_recv()

    def part(t, slot, q):
        if q == VECTOR:
            return vecs.at[t, :, pl.ds(slot * nb, nb)]
        return panel.at[t, pl.ds(slot * nb + q * quarter, quarter)]

    def own_part(t, q):
        if q == VECTOR:
            return own_vec.at[t - 3]
        return gath.at[t, pl.ds(q * quarter, quarter), own_lanes]

    def p_copy(t, q, src, slot, dev):
        return copy(src, part(t, slot, q), ps_sem.at[t, slot, q], pr_sem.at[t, slot, q], dev)

    def local_sends(t, q):
        return [p_copy(t, q, part(t, 0, q), 1, at(row_=sibling)), p_copy(t, q, part(t, 0, q), 2, at(row_=across))]

    def next_sends(q):
        src = own_part(3, q)
        return [p_copy(3, q, src, 0, at(dloop=1)), p_copy(3, q, src, 2, at(dloop=1, row_=across))]

    def relay_part(q):
        return relay.at[pl.ds(q * quarter, quarter)]

    def relay_send(q):
        return copy(own_part(3, q), relay_part(q), rs_sem.at[q], rr_sem.at[q], at(dloop=2))

    def relay_passes(q):
        src = relay_part(q)
        return [p_copy(3, q, src, 0, at(dloop=-1)), p_copy(3, q, src, 2, at(dloop=-1, row_=across))]

    def far_send(q):
        return p_copy(4, q, own_part(4, q), 0, at(dloop=2))

    def to_sibling(t, q, slot):
        return copy(part(t, slot, q), part(t, slot + 1, q), fs_sem.at[t, slot // 2, q], pr_sem.at[t, slot + 1, q], at(row_=sibling))

    def p_recv(t, slot, q):
        p_copy(t, q, part(t, slot, q), slot, at(row_=sibling)).wait_recv()

    def far_forward(t, q):
        p_recv(t, 2, q)
        to_sibling(t, q, 2).start()

    def join_part(t, q):
        p_recv(t, 1, q)
        p_recv(t, 3, q)

    def join(t):
        for q in range(5):
            join_part(t, q)

    def start_next(q):
        if q not in RELAYED:
            for c in next_sends(q):
                c.start()
            return

        @pl.when(even)
        def _():
            for c in next_sends(q):
                c.start()

        @pl.when(odd)
        def _():
            relay_send(q).start()

    def pass_relay(q):
        @pl.when(odd)
        def _():
            relay_send(q).wait_recv()
            for c in relay_passes(q):
                c.start()

    def make_hot(s):
        for slot, dcol in enumerate((0, n_col - 1, 1, 2)):
            start = pl.multiple_of(lax.rem(col + dcol, n_col) * nb, nb)
            q = pivs[pl.ds(s, 1), pl.ds(start, nb)]

            def one(row_slot, carry):
                base = lax.rem(row + 2 * lax.div(row_slot, 2), n_row)
                base = base + (1 - 2 * lax.rem(base, 2)) * lax.rem(row_slot, 2)
                iota = lax.broadcasted_iota(jnp.int16, (nb, nb), 0)
                wanted = jnp.broadcast_to((q - base * nb).astype(jnp.int16), (nb, nb))
                rows = pl.ds(pl.multiple_of(row_slot * nb, nb), nb)
                hot[rows, pl.ds(slot * nb, nb)] = jnp.where(iota == wanted, BF(1), BF(0))
                return carry

            lax.fori_loop(0, 4, one, 0)

    def permute(j, lanes, first):
        s, h = lax.div(j, 2), lax.rem(j, 2)
        rows = pl.ds(pl.multiple_of(h * half, half), half)

        def one(part_, carry):
            targets = pl.ds(pl.multiple_of(part_ * 2 * nb, 2 * nb), 2 * nb)
            moved = lax.dot_general(gath[s, rows, lanes], hot[targets, lanes], NT, preferred_element_type=F32).astype(BF)
            if first:
                perm[rows, targets] = moved
            else:
                perm[rows, targets] += moved
            return carry

        lax.fori_loop(0, 2, one, 0)

    def product(s, h):
        rows = pl.ds(pl.multiple_of(h * half, half), half)
        value = jnp.dot(perm[rows, :], panel[s], preferred_element_type=F32).astype(BF)

        @pl.when(s == 0)
        def _():
            panel[2, rows, :] = value

        @pl.when((s >= 1) & (s < 4))
        def _():
            gath[s + 1, rows, own_lanes] = value

        @pl.when(s == 4)
        def _():
            out_ref[rows, :] = value

    def finish_vector(s):
        rbuf[...] = lax.dot_general(vecs[s], perm[...], NT, preferred_element_type=F32)

        @pl.when(s < 2)
        def _():
            rbuf[...] += gbuf[pl.ds(2 * s + 1, 1), :]

        @pl.when(s == 0)
        def _():
            vecs[2, :, own_lanes] = rbuf[...].astype(BF)

        @pl.when(s == 1)
        def _():
            held[...] = rbuf[...]

        @pl.when(s == 2)
        def _():
            rbuf[...] += held[...]

        @pl.when(s >= 3)
        def _():
            rbuf[...] += own_vec[s - 3].astype(F32)

        @pl.when((s >= 2) & (s < 4))
        def _():
            own_vec[s - 2] = rbuf[...].astype(BF)

    loads = []
    for s in range(2):
        loads.append(pltpu.make_async_copy(w_ref.at[2 * s + 1], gath.at[s, :, own_lanes], load_sem.at[2 * s]))
        loads.append(pltpu.make_async_copy(w_ref.at[2 * s], panel.at[s, pl.ds(0, nb)], load_sem.at[2 * s + 1]))
    for load in loads:
        load.start()
    barrier = pltpu.get_barrier_semaphore()
    partners = (
        at(dcol=1), at(dcol=-1), at(dcol=2), at(row_=sibling), at(row_=across),
        at(dloop=1), at(dloop=-1), at(dloop=1, row_=across), at(dloop=-1, row_=across), at(dloop=2), at(dloop=-2),
    )
    for partner in partners:
        pl.semaphore_signal(barrier, inc=1, device_id=partner, device_id_type=MESH)
    own_cols = pl.ds(pl.multiple_of(col * share, share), share)
    gsend[...] = jnp.zeros_like(gsend)
    gsend[pl.ds(0, 4), :] = res_ref[...].astype(F32)
    gbuf[:, own_cols] = gsend[...]
    for s, interval in enumerate((0, 2, 1)):
        pivs[pl.ds(s, 1), :] = ipiv_ref[interval]
    pivs[pl.ds(3, 1), :] = bpiv_ref[pl.ds(loop, 1), :]
    pivs[pl.ds(4, 1), :] = bpiv_ref[pl.ds(lax.rem(loop + n_loop - 1, n_loop), 1), :]
    for load in loads:
        load.wait()
    pl.semaphore_wait(barrier, len(partners))

    def g_copy(i, dcol, holder):
        cols = pl.ds(pl.multiple_of(lax.rem(col + holder + n_col, n_col) * share, share), share)
        return copy(gsend, gbuf.at[:, cols], gs_sem.at[i], gr_sem.at[i], at(dcol=dcol))

    for j in (0, 1):
        y_issue(j, FIRST)
        y_issue(j, SECOND)
    for i, dcol in enumerate((1, -1, 2)):
        g_copy(i, dcol, 0).start()
    for q in range(4):
        for c in local_sends(0, q):
            c.start()
    make_hot(0)
    for i, dcol in enumerate((-1, 1, 2)):
        g_copy(i, dcol, dcol).wait_recv()
    for s in (0, 1):
        vecs[s, :, own_lanes] = jnp.broadcast_to(gbuf[pl.ds(2 * s, 1), :], (16, nb)).astype(BF)
    for c in local_sends(0, VECTOR):
        c.start()

    def drain(j, carry):
        for k in (FIRST, SECOND, PASSED):
            for direction in (0, 1):
                y_copy(j, k, direction).wait_send()
        return carry

    def drain_panel(t, carry):
        for q in range(5):
            for c in local_sends(t, q):
                c.wait_send()
            to_sibling(t, q, 2).wait_send()
        return carry

    def drain_next():
        for q in range(5):
            for slot in (0, 2):
                to_sibling(3, q, slot).wait_send()
            for c in next_sends(q):
                c.wait_send()

        @pl.when(odd)
        def _():
            for q in RELAYED:
                relay_send(q).wait_send()

    def step(j, carry):
        s, h = lax.div(j, 2), lax.rem(j, 2)

        def on(number, *actions):
            @pl.when(j == number)
            def _():
                for action, qs in actions:
                    for q in qs:
                        action(q)

        def first_far(q):
            far_forward(0, q)
            for c in local_sends(1, q):
                c.start()

        def second_far(q):
            far_forward(1, q)

        def third_far(q):
            far_forward(2, q)

        def pass_next(q):
            for slot in (0, 2):
                p_recv(3, slot, q)
                to_sibling(3, q, slot).start()

        def receive_far(q):
            p_recv(4, 0, q)
            for c in local_sends(4, q):
                c.start()

        def last_far(q):
            far_forward(4, q)

        @pl.when((j == 0) | (j == 6) | (j == 8))
        def _():
            y_recv(j, FIRST)
            y_issue(j, PASSED)

        on(6, (pass_next, (0,)))
        on(8, (receive_far, (0,)))

        @pl.when((j == 2) | (j == 4) | (j == 6))
        def _():
            make_hot(s)

        permute(j, own_lanes, True)
        on(8, (receive_far, (1,)))
        y_recv(j, SECOND)
        for last, new in ((0, 2), (1, 3)):
            @pl.when(j == last)
            def _():
                y_issue(new, FIRST)
                y_issue(new, SECOND)

        on(6, (pass_next, (1,)), (pass_relay, (2,)))
        on(7, (pass_next, (2,)))
        on(8, (receive_far, (2,)))
        on(9, (last_far, (2,)))

        @pl.when(j == 8)
        def _():
            y_recv(9, FIRST)
            y_issue(9, PASSED)

        permute(j, pl.ds(nb, 2 * nb), False)
        on(0, (first_far, (0, 1, 2, 3, VECTOR)))
        on(1, (second_far, (0, 1)))
        on(2, (second_far, (2, 3, VECTOR)))
        on(3, (third_far, (0, 1, 2, 3, VECTOR)))
        on(5, (pass_relay, (0,)))
        on(7, (pass_next, (3, VECTOR)))
        on(8, (receive_far, (3, VECTOR)), (last_far, (0,)))
        on(9, (last_far, (3, VECTOR)))
        @pl.when((j < 5) | (j == 6))
        def _():
            y_recv(j + 1, FIRST)
            y_issue(j + 1, PASSED)

        y_recv(j, PASSED)
        permute(j, pl.ds(3 * nb, nb), False)
        on(8, (last_far, (1,)))

        @pl.when((h == 0) & (s < 3))
        def _():
            join(s)


        on(7, (join, (3,)))

        @pl.when(j == 9)
        def _():
            join_part(4, VECTOR)
            finish_vector(4)
            lax.fori_loop(0, HALVES - 1, drain, 0)
            lax.fori_loop(0, 3, drain_panel, 0)
            drain_next()
            for q in range(VECTOR):
                join_part(4, q)

        def multiply(hh, carry):
            product(s, hh)
            return carry

        low = jnp.where(s < 3, h, 0)
        high = jnp.where((s < 3) | (h == 1), h + 1, 0)
        lax.fori_loop(low, high, multiply, 0)

        for done, new in ((2, (4,)), (3, (5,)), (4, (6,)), (5, (7,)), (7, (8, 9))):
            @pl.when(j == done)
            def _():
                for n in new:
                    y_issue(n, FIRST)
                    y_issue(n, SECOND)

        def start_third(q):
            for c in local_sends(2, q):
                c.start()

        def start_far(q):
            far_send(q).start()

        on(0, (start_third, (0, 1)))
        on(1, (start_third, (2, 3)))
        on(4, (start_next, (0, 1)))
        on(5, (start_next, (2, 3)))
        on(7, (start_far, (0, 1, 2, 3)))

        @pl.when((h == 1) & (s < 4))
        def _():
            finish_vector(s)

        on(1, (start_third, (VECTOR,)))
        on(5, (start_next, (VECTOR,)))
        on(7, (start_far, (VECTOR,)), (make_hot, (4,)))
        return carry

    lax.fori_loop(0, HALVES, step, 0)
    rhs_ref[...] = rbuf[pl.ds(0, 1), own_cols]

    for i, dcol in enumerate((1, -1, 2)):
        g_copy(i, dcol, 0).wait_send()
    drain(HALVES - 1, 0)
    drain_panel(4, 0)
    for q in range(5):
        far_send(q).wait_send()


def deliver(block_ref, rhs_ref, block_out, rhs_out, sems):
    copies = [
        pltpu.make_async_copy(block_ref, block_out, sems.at[0]),
        pltpu.make_async_copy(rhs_ref, rhs_out, sems.at[1]),
    ]
    for copy in copies:
        copy.start()
    for copy in copies:
        copy.wait()


def shards(interval_blocks, interval_pivots, boundary_pivots, interval_residuals):
    blocks, residuals = interval_blocks[0], interval_residuals[0]
    nb, share = blocks.shape[1], residuals.shape[1]
    vmem = pl.BlockSpec(memory_space=pltpu.VMEM)
    reduced, rhs = pl.pallas_call(
        body,
        out_shape=(jax.ShapeDtypeStruct((nb, nb), BF), jax.ShapeDtypeStruct((1, share), F32)),
        in_specs=[pl.BlockSpec(memory_space=pl.ANY)] + [vmem] * 3,
        out_specs=(vmem, vmem),
        scratch_shapes=[
            pltpu.VMEM((STAGES, nb, 4 * nb), BF),
            pltpu.VMEM((STAGES, 4 * nb, nb), BF),
            pltpu.VMEM((STAGES, 16, 4 * nb), BF),
            pltpu.VMEM((2, 16, nb), BF),
            pltpu.VMEM((nb, nb), BF),
            pltpu.VMEM((nb, 4 * nb), BF),
            pltpu.VMEM((4 * nb, 4 * nb), BF),
            pltpu.VMEM((8, 4 * nb), jnp.int32),
            pltpu.VMEM((8, share), F32),
            pltpu.VMEM((8, nb), F32),
            pltpu.VMEM((16, nb), F32),
            pltpu.VMEM((16, nb), F32),
            pltpu.SemaphoreType.DMA((4,)),
            pltpu.SemaphoreType.DMA((3,)),
            pltpu.SemaphoreType.DMA((3,)),
            pltpu.SemaphoreType.DMA((HALVES, 3, 2)),
            pltpu.SemaphoreType.DMA((HALVES, 3, 2)),
            pltpu.SemaphoreType.DMA((STAGES, 4, 5)),
            pltpu.SemaphoreType.DMA((STAGES, 4, 5)),
            pltpu.SemaphoreType.DMA((5,)),
            pltpu.SemaphoreType.DMA((5,)),
            pltpu.SemaphoreType.DMA((STAGES, 2, 5)),
        ],
        compiler_params=pltpu.CompilerParams(
            collective_id=0, has_side_effects=True, vmem_limit_bytes=60 * 2**20
        ),
        name="newton",
    )(blocks, jnp.transpose(interval_pivots, (1, 0, 2)), boundary_pivots, residuals)
    anywhere = pl.BlockSpec(memory_space=pl.ANY)
    reduced, rhs = pl.pallas_call(
        deliver,
        out_shape=(jax.ShapeDtypeStruct((nb, nb), BF), jax.ShapeDtypeStruct((1, share), F32)),
        in_specs=[anywhere] * 2,
        out_specs=(anywhere, anywhere),
        scratch_shapes=[pltpu.SemaphoreType.DMA((2,))],
        name="deliver",
    )(reduced, rhs)
    return reduced[None], rhs


def solution(mesh):
    placed = (
        P("loop", None, "row", "col"),
        P("loop", None, None),
        P(),
        P("loop", None, ("row", "col")),
    )
    return jax.shard_map(
        shards,
        mesh=mesh,
        in_specs=placed,
        out_specs=(P("loop", "row", "col"), P("loop", ("row", "col"))),
        check_vma=False,
    )
```

```python
import jax
import jax.numpy as jnp
from jax import lax
from jax.experimental import pallas as pl
from jax.experimental.pallas import tpu as pltpu
from jax.sharding import PartitionSpec as P

MESH = pl.DeviceIdType.MESH
BF, F32 = jnp.bfloat16, jnp.float32
NT = (((1,), (1,)), ((), ()))

FIRST, SECOND, PASSED = 0, 1, 2
STAGES, HALVES, VECTOR = 5, 10, 4


def body(w_ref, ipiv_hbm, bpiv_hbm, res_hbm, out_ref, rhs_ref, ipiv_ref, bpiv_ref, res_ref, gath, panel, vecs, own_vec, relay, relay_vec, perm, hot, pivs,
         gsend, gbuf, rbuf, held, load_sem, gs_sem, gr_sem, ys_sem, yr_sem, ps_sem, pr_sem, rs_sem, rr_sem, fs_sem):
    loop, row, col = lax.axis_index("loop"), lax.axis_index("row"), lax.axis_index("col")
    n_loop, n_row, n_col = lax.axis_size("loop"), lax.axis_size("row"), lax.axis_size("col")
    nb = perm.shape[0]
    half, quarter = nb // 2, nb // 4
    share = res_ref.shape[1]
    odd = lax.rem(loop, 2) == 1
    even = lax.rem(loop, 2) == 0
    own_lanes = pl.ds(0, nb)

    def at(dloop=0, row_=None, dcol=0):
        return {
            "loop": lax.rem(loop + dloop + n_loop, n_loop),
            "row": row if row_ is None else row_,
            "col": lax.rem(col + dcol + n_col, n_col),
        }

    sibling = row + 1 - 2 * lax.rem(row, 2)
    across = lax.rem(row + 2, n_row)

    def copy(src, dst, ssem, rsem, dev):
        return pltpu.make_async_remote_copy(
            src_ref=src, dst_ref=dst, send_sem=ssem, recv_sem=rsem, device_id=dev, device_id_type=MESH
        )

    def y_copy(j, k, direction):
        s, h = lax.div(j, 2), lax.rem(j, 2)
        near = 1 + direction
        offset = (direction + (k == SECOND)) % 2 * quarter
        rows = pl.ds(pl.multiple_of(h * half + offset, quarter), quarter)
        near_lanes = pl.ds(near * nb, nb)
        if k == PASSED:
            src, dst = gath.at[s, rows, near_lanes], gath.at[s, rows, pl.ds(3 * nb, nb)]
        else:
            src, dst = gath.at[s, rows, own_lanes], gath.at[s, rows, near_lanes]
        return copy(src, dst, ys_sem.at[j, k, direction], yr_sem.at[j, k, direction], at(dcol=1 - 2 * direction))

    def y_issue(j, k):
        for direction in (0, 1):
            y_copy(j, k, direction).start()

    def y_recv(j, k):
        for direction in (0, 1):
            y_copy(j, k, direction).wait_recv()

    def part(t, slot, q):
        if q == VECTOR:
            return vecs.at[t, :, pl.ds(slot * nb, nb)]
        return panel.at[t, pl.ds(slot * nb + q * quarter, quarter)]

    def own_part(t, q):
        if q == VECTOR:
            return own_vec.at[t - 3]
        return gath.at[t, pl.ds(q * quarter, quarter), own_lanes]

    def p_copy(t, q, src, slot, dev):
        return copy(src, part(t, slot, q), ps_sem.at[t, slot, q], pr_sem.at[t, slot, q], dev)

    def local_sends(t, q):
        return [p_copy(t, q, part(t, 0, q), 1, at(row_=sibling)), p_copy(t, q, part(t, 0, q), 2, at(row_=across))]

    def next_sends(q):
        src = own_part(3, q)
        return [p_copy(3, q, src, 0, at(dloop=1)), p_copy(3, q, src, 2, at(dloop=1, row_=across))]

    def relay_part(q):
        return relay_vec if q == VECTOR else relay.at[pl.ds(q * quarter, quarter)]

    def relay_send(q):
        return copy(own_part(3, q), relay_part(q), rs_sem.at[q], rr_sem.at[q], at(dloop=2))

    def relay_passes(q):
        src = relay_part(q)
        return [p_copy(3, q, src, 0, at(dloop=-1)), p_copy(3, q, src, 2, at(dloop=-1, row_=across))]

    def far_send(q):
        return p_copy(4, q, own_part(4, q), 0, at(dloop=2))

    def to_sibling(t, q, slot):
        return copy(part(t, slot, q), part(t, slot + 1, q), fs_sem.at[t, slot // 2, q], pr_sem.at[t, slot + 1, q], at(row_=sibling))

    def p_recv(t, slot, q):
        p_copy(t, q, part(t, slot, q), slot, at(row_=sibling)).wait_recv()

    def far_forward(t, q):
        p_recv(t, 2, q)
        to_sibling(t, q, 2).start()

    def join_part(t, q):
        p_recv(t, 1, q)
        p_recv(t, 3, q)

    def join(t):
        for q in range(5):
            join_part(t, q)

    def start_next(q):
        @pl.when(even)
        def _():
            for c in next_sends(q):
                c.start()

        @pl.when(odd)
        def _():
            relay_send(q).start()

    def pass_relay(q):
        @pl.when(odd)
        def _():
            relay_send(q).wait_recv()
            for c in relay_passes(q):
                c.start()

    def make_hot(s):
        for slot, dcol in enumerate((0, n_col - 1, 1, 2)):
            start = pl.multiple_of(lax.rem(col + dcol, n_col) * nb, nb)
            q = pivs[pl.ds(s, 1), pl.ds(start, nb)]

            def one(row_slot, carry):
                base = lax.rem(row + 2 * lax.div(row_slot, 2), n_row)
                base = base + (1 - 2 * lax.rem(base, 2)) * lax.rem(row_slot, 2)
                iota = lax.broadcasted_iota(jnp.int16, (nb, nb), 0)
                wanted = jnp.broadcast_to((q - base * nb).astype(jnp.int16), (nb, nb))
                rows = pl.ds(pl.multiple_of(row_slot * nb, nb), nb)
                hot[rows, pl.ds(slot * nb, nb)] = jnp.where(iota == wanted, BF(1), BF(0))
                return carry

            lax.fori_loop(0, 4, one, 0)

    def permute(j, lanes, first):
        s, h = lax.div(j, 2), lax.rem(j, 2)
        rows = pl.ds(pl.multiple_of(h * half, half), half)

        def one(part_, carry):
            targets = pl.ds(pl.multiple_of(part_ * 2 * nb, 2 * nb), 2 * nb)
            moved = lax.dot_general(gath[s, rows, lanes], hot[targets, lanes], NT, preferred_element_type=F32).astype(BF)
            if first:
                perm[rows, targets] = moved
            else:
                perm[rows, targets] += moved
            return carry

        lax.fori_loop(0, 2, one, 0)

    def product(s, h):
        rows = pl.ds(pl.multiple_of(h * half, half), half)
        value = jnp.dot(perm[rows, :], panel[s], preferred_element_type=F32).astype(BF)

        @pl.when(s == 0)
        def _():
            panel[2, rows, :] = value

        @pl.when((s >= 1) & (s < 4))
        def _():
            gath[s + 1, rows, own_lanes] = value

        @pl.when(s == 4)
        def _():
            out_ref[rows, :] = value

    def finish_vector(s):
        rbuf[...] = lax.dot_general(vecs[s], perm[...], NT, preferred_element_type=F32)

        @pl.when(s < 2)
        def _():
            rbuf[...] += gbuf[pl.ds(2 * s + 1, 1), :]

        @pl.when(s == 0)
        def _():
            vecs[2, :, own_lanes] = rbuf[...].astype(BF)

        @pl.when(s == 1)
        def _():
            held[...] = rbuf[...]

        @pl.when(s == 2)
        def _():
            rbuf[...] += held[...]

        @pl.when(s >= 3)
        def _():
            rbuf[...] += own_vec[s - 3].astype(F32)

        @pl.when((s >= 2) & (s < 4))
        def _():
            own_vec[s - 2] = rbuf[...].astype(BF)

    loads = []
    for s in range(2):
        loads.append(pltpu.make_async_copy(w_ref.at[2 * s + 1], gath.at[s, :, own_lanes], load_sem.at[2 * s]))
        loads.append(pltpu.make_async_copy(w_ref.at[2 * s], panel.at[s, pl.ds(0, nb)], load_sem.at[2 * s + 1]))
    small = [
        pltpu.make_async_copy(src, dst, load_sem.at[4 + i])
        for i, (src, dst) in enumerate(((ipiv_hbm, ipiv_ref), (bpiv_hbm, bpiv_ref), (res_hbm, res_ref)))
    ]
    for load in small + loads:
        load.start()
    barrier = pltpu.get_barrier_semaphore()
    partners = (
        at(dcol=1), at(dcol=-1), at(dcol=2), at(row_=sibling), at(row_=across),
        at(dloop=1), at(dloop=-1), at(dloop=1, row_=across), at(dloop=-1, row_=across), at(dloop=2), at(dloop=-2),
    )
    for partner in partners:
        pl.semaphore_signal(barrier, inc=1, device_id=partner, device_id_type=MESH)
    own_cols = pl.ds(pl.multiple_of(col * share, share), share)
    for load in small:
        load.wait()
    gsend[...] = jnp.zeros_like(gsend)
    gsend[pl.ds(0, 4), :] = res_ref[...].astype(F32)
    gbuf[:, own_cols] = gsend[...]
    for s, interval in enumerate((0, 2, 1)):
        pivs[pl.ds(s, 1), :] = ipiv_ref[interval]
    pivs[pl.ds(3, 1), :] = bpiv_ref[pl.ds(loop, 1), :]
    pivs[pl.ds(4, 1), :] = bpiv_ref[pl.ds(lax.rem(loop + n_loop - 1, n_loop), 1), :]
    for load in loads:
        load.wait()
    pl.semaphore_wait(barrier, len(partners))

    def g_copy(i, dcol, holder):
        cols = pl.ds(pl.multiple_of(lax.rem(col + holder + n_col, n_col) * share, share), share)
        return copy(gsend, gbuf.at[:, cols], gs_sem.at[i], gr_sem.at[i], at(dcol=dcol))

    for j in (0, 1):
        y_issue(j, FIRST)
        y_issue(j, SECOND)
    for i, dcol in enumerate((1, -1, 2)):
        g_copy(i, dcol, 0).start()
    for q in range(4):
        for c in local_sends(0, q):
            c.start()
    make_hot(0)
    for i, dcol in enumerate((-1, 1, 2)):
        g_copy(i, dcol, dcol).wait_recv()
    for s in (0, 1):
        vecs[s, :, own_lanes] = jnp.broadcast_to(gbuf[pl.ds(2 * s, 1), :], (16, nb)).astype(BF)
    for c in local_sends(0, VECTOR):
        c.start()

    def drain(j, carry):
        for k in (FIRST, SECOND, PASSED):
            for direction in (0, 1):
                y_copy(j, k, direction).wait_send()
        return carry

    def drain_panel(t, carry):
        for q in range(5):
            for c in local_sends(t, q):
                c.wait_send()
            to_sibling(t, q, 2).wait_send()
        return carry

    def drain_next():
        for q in range(5):
            for slot in (0, 2):
                to_sibling(3, q, slot).wait_send()
            for c in next_sends(q):
                c.wait_send()

        @pl.when(odd)
        def _():
            for q in range(5):
                relay_send(q).wait_send()

    def step(j, carry):
        s, h = lax.div(j, 2), lax.rem(j, 2)

        def on(number, *actions):
            @pl.when(j == number)
            def _():
                for action, qs in actions:
                    for q in qs:
                        action(q)

        def first_far(q):
            far_forward(0, q)
            for c in local_sends(1, q):
                c.start()

        def second_far(q):
            far_forward(1, q)

        def third_far(q):
            far_forward(2, q)

        def pass_next(q):
            for slot in (0, 2):
                p_recv(3, slot, q)
                to_sibling(3, q, slot).start()

        def receive_far(q):
            p_recv(4, 0, q)
            for c in local_sends(4, q):
                c.start()

        def last_far(q):
            far_forward(4, q)

        @pl.when((j == 0) | (j == 6) | (j == 8))
        def _():
            y_recv(j, FIRST)
            y_issue(j, PASSED)

        on(6, (pass_relay, (1,)), (pass_next, (0,)))
        on(8, (receive_far, (0,)))

        @pl.when((j == 2) | (j == 4) | (j == 6))
        def _():
            make_hot(s)

        permute(j, own_lanes, True)
        on(8, (receive_far, (1,)))
        y_recv(j, SECOND)
        for last, new in ((0, 2), (1, 3)):
            @pl.when(j == last)
            def _():
                y_issue(new, FIRST)
                y_issue(new, SECOND)

        on(6, (pass_next, (1,)), (pass_relay, (2,)))
        on(7, (pass_next, (2,)))
        on(8, (receive_far, (2,)))
        on(9, (last_far, (2,)))

        @pl.when(j == 8)
        def _():
            y_recv(9, FIRST)
            y_issue(9, PASSED)

        permute(j, pl.ds(nb, 2 * nb), False)
        on(0, (first_far, (0, 1, 2, 3, VECTOR)))
        on(1, (second_far, (0, 1)))
        on(2, (second_far, (2, 3, VECTOR)))
        on(3, (third_far, (0, 1, 2, 3, VECTOR)))
        on(5, (pass_relay, (0,)))
        on(6, (pass_relay, (3, VECTOR)))
        on(7, (pass_next, (3, VECTOR)))
        on(8, (receive_far, (3, VECTOR)), (last_far, (0,)))
        on(9, (last_far, (3, VECTOR)))
        @pl.when((j < 5) | (j == 6))
        def _():
            y_recv(j + 1, FIRST)
            y_issue(j + 1, PASSED)

        y_recv(j, PASSED)
        permute(j, pl.ds(3 * nb, nb), False)
        on(8, (last_far, (1,)))

        @pl.when((h == 0) & (s < 3))
        def _():
            join(s)


        on(7, (join, (3,)))

        @pl.when(j == 9)
        def _():
            join_part(4, VECTOR)
            finish_vector(4)
            lax.fori_loop(0, HALVES - 1, drain, 0)
            lax.fori_loop(0, 3, drain_panel, 0)
            drain_next()
            for q in range(VECTOR):
                join_part(4, q)

        def multiply(hh, carry):
            product(s, hh)
            return carry

        low = jnp.where(s < 3, h, 0)
        high = jnp.where((s < 3) | (h == 1), h + 1, 0)
        lax.fori_loop(low, high, multiply, 0)

        for done, new in ((2, (4,)), (3, (5,)), (4, (6,)), (5, (7,)), (7, (8, 9))):
            @pl.when(j == done)
            def _():
                for n in new:
                    y_issue(n, FIRST)
                    y_issue(n, SECOND)

        def start_third(q):
            for c in local_sends(2, q):
                c.start()

        def start_far(q):
            far_send(q).start()

        on(0, (start_third, (0, 1)))
        on(1, (start_third, (2, 3)))
        on(4, (start_next, (0, 1)))
        on(5, (start_next, (2, 3)))
        on(7, (start_far, (0, 1, 2, 3)))

        @pl.when((h == 1) & (s < 4))
        def _():
            finish_vector(s)

        on(1, (start_third, (VECTOR,)))
        on(5, (start_next, (VECTOR,)))
        on(7, (start_far, (VECTOR,)), (make_hot, (4,)))
        return carry

    lax.fori_loop(0, HALVES, step, 0)
    rhs_ref[...] = rbuf[pl.ds(0, 1), own_cols]

    for i, dcol in enumerate((1, -1, 2)):
        g_copy(i, dcol, 0).wait_send()
    drain(HALVES - 1, 0)
    drain_panel(4, 0)
    for q in range(5):
        far_send(q).wait_send()


def deliver(block_ref, rhs_ref, block_out, rhs_out, sems):
    copies = [
        pltpu.make_async_copy(block_ref, block_out, sems.at[0]),
        pltpu.make_async_copy(rhs_ref, rhs_out, sems.at[1]),
    ]
    for copy in copies:
        copy.start()
    for copy in copies:
        copy.wait()


def shards(interval_blocks, interval_pivots, boundary_pivots, interval_residuals):
    blocks, residuals = interval_blocks[0], interval_residuals[0]
    nb, share = blocks.shape[1], residuals.shape[1]
    vmem = pl.BlockSpec(memory_space=pltpu.VMEM)
    anywhere = pl.BlockSpec(memory_space=pl.ANY)
    interval_rows = jnp.transpose(interval_pivots, (1, 0, 2))
    reduced, rhs = pl.pallas_call(
        body,
        out_shape=(jax.ShapeDtypeStruct((nb, nb), BF), jax.ShapeDtypeStruct((1, share), F32)),
        in_specs=[anywhere] * 4,
        out_specs=(vmem, vmem),
        scratch_shapes=[
            pltpu.VMEM(interval_rows.shape, jnp.int32),
            pltpu.VMEM(boundary_pivots.shape, jnp.int32),
            pltpu.VMEM(residuals.shape, BF),
            pltpu.VMEM((STAGES, nb, 4 * nb), BF),
            pltpu.VMEM((STAGES, 4 * nb, nb), BF),
            pltpu.VMEM((STAGES, 16, 4 * nb), BF),
            pltpu.VMEM((2, 16, nb), BF),
            pltpu.VMEM((nb, nb), BF),
            pltpu.VMEM((16, nb), BF),
            pltpu.VMEM((nb, 4 * nb), BF),
            pltpu.VMEM((4 * nb, 4 * nb), BF),
            pltpu.VMEM((8, 4 * nb), jnp.int32),
            pltpu.VMEM((8, share), F32),
            pltpu.VMEM((8, nb), F32),
            pltpu.VMEM((16, nb), F32),
            pltpu.VMEM((16, nb), F32),
            pltpu.SemaphoreType.DMA((7,)),
            pltpu.SemaphoreType.DMA((3,)),
            pltpu.SemaphoreType.DMA((3,)),
            pltpu.SemaphoreType.DMA((HALVES, 3, 2)),
            pltpu.SemaphoreType.DMA((HALVES, 3, 2)),
            pltpu.SemaphoreType.DMA((STAGES, 4, 5)),
            pltpu.SemaphoreType.DMA((STAGES, 4, 5)),
            pltpu.SemaphoreType.DMA((5,)),
            pltpu.SemaphoreType.DMA((5,)),
            pltpu.SemaphoreType.DMA((STAGES, 2, 5)),
        ],
        compiler_params=pltpu.CompilerParams(
            collective_id=0, has_side_effects=True, vmem_limit_bytes=60 * 2**20
        ),
        name="newton",
    )(blocks, interval_rows, boundary_pivots, residuals)
    reduced, rhs = pl.pallas_call(
        deliver,
        out_shape=(jax.ShapeDtypeStruct((nb, nb), BF), jax.ShapeDtypeStruct((1, share), F32)),
        in_specs=[anywhere] * 2,
        out_specs=(vmem, vmem),
        scratch_shapes=[pltpu.SemaphoreType.DMA((2,))],
        name="deliver",
    )(reduced, rhs)
    return reduced[None], rhs


def solution(mesh):
    placed = (
        P("loop", None, "row", "col"),
        P("loop", None, None),
        P(),
        P("loop", None, ("row", "col")),
    )
    return jax.shard_map(
        shards,
        mesh=mesh,
        in_specs=placed,
        out_specs=(P("loop", "row", "col"), P("loop", ("row", "col"))),
        check_vma=False,
    )
```

```python
import jax
import jax.numpy as jnp
from jax import lax
from jax.experimental import pallas as pl
from jax.experimental.pallas import tpu as pltpu
from jax.sharding import PartitionSpec as P

MESH = pl.DeviceIdType.MESH
BF, F32 = jnp.bfloat16, jnp.float32
NT = (((1,), (1,)), ((), ()))

FIRST, SECOND, PASSED = 0, 1, 2
STAGES, HALVES, VECTOR = 5, 10, 4


def body(w_ref, ipiv_hbm, bpiv_hbm, res_hbm, out_ref, rhs_ref, ipiv_ref, bpiv_ref, res_ref, gath, panel, vecs, own_vec, relay, relay_vec, perm, hot, pivs,
         gsend, gbuf, rbuf, held, load_sem, gs_sem, gr_sem, ys_sem, yr_sem, ps_sem, pr_sem, rs_sem, rr_sem, fs_sem):
    loop, row, col = lax.axis_index("loop"), lax.axis_index("row"), lax.axis_index("col")
    n_loop, n_row, n_col = lax.axis_size("loop"), lax.axis_size("row"), lax.axis_size("col")
    nb = perm.shape[0]
    half, quarter = nb // 2, nb // 4
    share = res_ref.shape[1]
    odd = lax.rem(loop, 2) == 1
    even = lax.rem(loop, 2) == 0
    own_lanes = pl.ds(0, nb)

    def at(dloop=0, row_=None, dcol=0):
        return {
            "loop": lax.rem(loop + dloop + n_loop, n_loop),
            "row": row if row_ is None else row_,
            "col": lax.rem(col + dcol + n_col, n_col),
        }

    sibling = row + 1 - 2 * lax.rem(row, 2)
    across = lax.rem(row + 2, n_row)

    def copy(src, dst, ssem, rsem, dev):
        return pltpu.make_async_remote_copy(
            src_ref=src, dst_ref=dst, send_sem=ssem, recv_sem=rsem, device_id=dev, device_id_type=MESH
        )

    def y_copy(j, k, direction):
        s, h = lax.div(j, 2), lax.rem(j, 2)
        near = 1 + direction
        offset = (direction + (k == SECOND)) % 2 * quarter
        rows = pl.ds(pl.multiple_of(h * half + offset, quarter), quarter)
        near_lanes = pl.ds(near * nb, nb)
        if k == PASSED:
            src, dst = gath.at[s, rows, near_lanes], gath.at[s, rows, pl.ds(3 * nb, nb)]
        else:
            src, dst = gath.at[s, rows, own_lanes], gath.at[s, rows, near_lanes]
        return copy(src, dst, ys_sem.at[j, k, direction], yr_sem.at[j, k, direction], at(dcol=1 - 2 * direction))

    def y_issue(j, k):
        for direction in (0, 1):
            y_copy(j, k, direction).start()

    def y_recv(j, k):
        for direction in (0, 1):
            y_copy(j, k, direction).wait_recv()

    def part(t, slot, q):
        if q == VECTOR:
            return vecs.at[t, :, pl.ds(slot * nb, nb)]
        return panel.at[t, pl.ds(slot * nb + q * quarter, quarter)]

    def own_part(t, q):
        if q == VECTOR:
            return own_vec.at[t - 3]
        return gath.at[t, pl.ds(q * quarter, quarter), own_lanes]

    def p_copy(t, q, src, slot, dev):
        return copy(src, part(t, slot, q), ps_sem.at[t, slot, q], pr_sem.at[t, slot, q], dev)

    def local_sends(t, q):
        return [p_copy(t, q, part(t, 0, q), 1, at(row_=sibling)), p_copy(t, q, part(t, 0, q), 2, at(row_=across))]

    def next_sends(q):
        src = own_part(3, q)
        return [p_copy(3, q, src, 0, at(dloop=1)), p_copy(3, q, src, 2, at(dloop=1, row_=across))]

    def relay_part(q):
        return relay_vec if q == VECTOR else relay.at[pl.ds(q * quarter, quarter)]

    def relay_send(q):
        return copy(own_part(3, q), relay_part(q), rs_sem.at[q], rr_sem.at[q], at(dloop=2))

    def relay_passes(q):
        src = relay_part(q)
        return [p_copy(3, q, src, 0, at(dloop=-1)), p_copy(3, q, src, 2, at(dloop=-1, row_=across))]

    def far_send(q):
        return p_copy(4, q, own_part(4, q), 0, at(dloop=2))

    def to_sibling(t, q, slot):
        return copy(part(t, slot, q), part(t, slot + 1, q), fs_sem.at[t, slot // 2, q], pr_sem.at[t, slot + 1, q], at(row_=sibling))

    def p_recv(t, slot, q):
        p_copy(t, q, part(t, slot, q), slot, at(row_=sibling)).wait_recv()

    def far_forward(t, q):
        p_recv(t, 2, q)
        to_sibling(t, q, 2).start()

    def join_part(t, q):
        p_recv(t, 1, q)
        p_recv(t, 3, q)

    def join(t):
        for q in range(5):
            join_part(t, q)

    def start_next(q):
        @pl.when(even)
        def _():
            for c in next_sends(q):
                c.start()

        @pl.when(odd)
        def _():
            relay_send(q).start()

    def pass_relay(q):
        @pl.when(odd)
        def _():
            relay_send(q).wait_recv()
            for c in relay_passes(q):
                c.start()

    def make_hot(s):
        for slot, dcol in enumerate((0, n_col - 1, 1, 2)):
            start = pl.multiple_of(lax.rem(col + dcol, n_col) * nb, nb)
            q = pivs[pl.ds(s, 1), pl.ds(start, nb)]

            def one(row_slot, carry):
                base = lax.rem(row + 2 * lax.div(row_slot, 2), n_row)
                base = base + (1 - 2 * lax.rem(base, 2)) * lax.rem(row_slot, 2)
                iota = lax.broadcasted_iota(jnp.int16, (nb, nb), 0)
                wanted = jnp.broadcast_to((q - base * nb).astype(jnp.int16), (nb, nb))
                rows = pl.ds(pl.multiple_of(row_slot * nb, nb), nb)
                hot[lax.rem(s, 2), rows, pl.ds(slot * nb, nb)] = jnp.where(iota == wanted, BF(1), BF(0))
                return carry

            lax.fori_loop(0, 4, one, 0)

    def permute(j, lanes, first):
        s, h = lax.div(j, 2), lax.rem(j, 2)
        rows = pl.ds(pl.multiple_of(h * half, half), half)

        def one(part_, carry):
            targets = pl.ds(pl.multiple_of(part_ * 2 * nb, 2 * nb), 2 * nb)
            moved = lax.dot_general(gath[s, rows, lanes], hot[lax.rem(s, 2), targets, lanes], NT, preferred_element_type=F32).astype(BF)
            if first:
                perm[rows, targets] = moved
            else:
                perm[rows, targets] += moved
            return carry

        lax.fori_loop(0, 2, one, 0)

    def product(s, h):
        rows = pl.ds(pl.multiple_of(h * half, half), half)
        value = jnp.dot(perm[rows, :], panel[s], preferred_element_type=F32).astype(BF)

        @pl.when(s == 0)
        def _():
            panel[2, rows, :] = value

        @pl.when((s >= 1) & (s < 4))
        def _():
            gath[s + 1, rows, own_lanes] = value

        @pl.when(s == 4)
        def _():
            out_ref[rows, :] = value

    def finish_vector(s):
        rbuf[...] = lax.dot_general(vecs[s], perm[...], NT, preferred_element_type=F32)

        @pl.when(s < 2)
        def _():
            rbuf[...] += gbuf[pl.ds(2 * s + 1, 1), :]

        @pl.when(s == 0)
        def _():
            vecs[2, :, own_lanes] = rbuf[...].astype(BF)

        @pl.when(s == 1)
        def _():
            held[...] = rbuf[...]

        @pl.when(s == 2)
        def _():
            rbuf[...] += held[...]

        @pl.when(s >= 3)
        def _():
            rbuf[...] += own_vec[s - 3].astype(F32)

        @pl.when((s >= 2) & (s < 4))
        def _():
            own_vec[s - 2] = rbuf[...].astype(BF)

    loads = []
    for s in range(2):
        loads.append(pltpu.make_async_copy(w_ref.at[2 * s + 1], gath.at[s, :, own_lanes], load_sem.at[2 * s]))
        loads.append(pltpu.make_async_copy(w_ref.at[2 * s], panel.at[s, pl.ds(0, nb)], load_sem.at[2 * s + 1]))
    small = [
        pltpu.make_async_copy(src, dst, load_sem.at[4 + i])
        for i, (src, dst) in enumerate(((ipiv_hbm, ipiv_ref), (bpiv_hbm, bpiv_ref), (res_hbm, res_ref)))
    ]
    for load in small + loads:
        load.start()
    barrier = pltpu.get_barrier_semaphore()
    partners = (
        at(dcol=1), at(dcol=-1), at(dcol=2), at(row_=sibling), at(row_=across),
        at(dloop=1), at(dloop=-1), at(dloop=1, row_=across), at(dloop=-1, row_=across), at(dloop=2), at(dloop=-2),
    )
    for partner in partners:
        pl.semaphore_signal(barrier, inc=1, device_id=partner, device_id_type=MESH)
    own_cols = pl.ds(pl.multiple_of(col * share, share), share)
    for load in small:
        load.wait()
    gsend[...] = jnp.zeros_like(gsend)
    gsend[pl.ds(0, 4), :] = res_ref[...].astype(F32)
    gbuf[:, own_cols] = gsend[...]
    for s, interval in enumerate((0, 2, 1)):
        pivs[pl.ds(s, 1), :] = ipiv_ref[interval]
    pivs[pl.ds(3, 1), :] = bpiv_ref[pl.ds(loop, 1), :]
    pivs[pl.ds(4, 1), :] = bpiv_ref[pl.ds(lax.rem(loop + n_loop - 1, n_loop), 1), :]
    for load in loads:
        load.wait()
    pl.semaphore_wait(barrier, len(partners))

    def g_copy(i, dcol, holder):
        cols = pl.ds(pl.multiple_of(lax.rem(col + holder + n_col, n_col) * share, share), share)
        return copy(gsend, gbuf.at[:, cols], gs_sem.at[i], gr_sem.at[i], at(dcol=dcol))

    for j in (0, 1):
        y_issue(j, FIRST)
        y_issue(j, SECOND)
    for i, dcol in enumerate((1, -1, 2)):
        g_copy(i, dcol, 0).start()
    for q in range(4):
        for c in local_sends(0, q):
            c.start()
    make_hot(0)
    for i, dcol in enumerate((-1, 1, 2)):
        g_copy(i, dcol, dcol).wait_recv()
    for s in (0, 1):
        vecs[s, :, own_lanes] = jnp.broadcast_to(gbuf[pl.ds(2 * s, 1), :], (16, nb)).astype(BF)
    for c in local_sends(0, VECTOR):
        c.start()

    def drain(j, carry):
        for k in (FIRST, SECOND, PASSED):
            for direction in (0, 1):
                y_copy(j, k, direction).wait_send()
        return carry

    def drain_panel(t, carry):
        for q in range(5):
            for c in local_sends(t, q):
                c.wait_send()
            to_sibling(t, q, 2).wait_send()
        return carry

    def drain_next():
        for q in range(5):
            for slot in (0, 2):
                to_sibling(3, q, slot).wait_send()
            for c in next_sends(q):
                c.wait_send()

        @pl.when(odd)
        def _():
            for q in range(5):
                relay_send(q).wait_send()

    def step(j, carry):
        s, h = lax.div(j, 2), lax.rem(j, 2)

        def on(number, *actions):
            @pl.when(j == number)
            def _():
                for action, qs in actions:
                    for q in qs:
                        action(q)

        def first_far(q):
            far_forward(0, q)
            for c in local_sends(1, q):
                c.start()

        def second_far(q):
            far_forward(1, q)

        def third_far(q):
            far_forward(2, q)

        def pass_next(q):
            for slot in (0, 2):
                p_recv(3, slot, q)
                to_sibling(3, q, slot).start()

        def receive_far(q):
            p_recv(4, 0, q)
            for c in local_sends(4, q):
                c.start()

        def last_far(q):
            far_forward(4, q)

        @pl.when((j == 0) | (j == 6) | (j == 8))
        def _():
            y_recv(j, FIRST)
            y_issue(j, PASSED)

        on(6, (pass_relay, (1,)), (pass_next, (0,)))
        on(8, (receive_far, (0,)))

        permute(j, own_lanes, True)
        on(8, (receive_far, (1,)))
        y_recv(j, SECOND)
        for last, new in ((0, 2), (1, 3)):
            @pl.when(j == last)
            def _():
                y_issue(new, FIRST)
                y_issue(new, SECOND)

        on(6, (pass_next, (1,)), (pass_relay, (2,)))
        on(7, (pass_next, (2,)))
        on(8, (receive_far, (2,)))
        on(9, (last_far, (2,)))

        @pl.when(j == 8)
        def _():
            y_recv(9, FIRST)
            y_issue(9, PASSED)

        permute(j, pl.ds(nb, 2 * nb), False)
        on(0, (first_far, (0, 1, 2, 3, VECTOR)))
        on(1, (second_far, (0, 1)))
        on(2, (second_far, (2, 3, VECTOR)))
        on(3, (third_far, (0, 1, 2, 3, VECTOR)))
        on(5, (pass_relay, (0,)))
        on(6, (pass_relay, (3, VECTOR)))
        on(7, (pass_next, (3, VECTOR)))
        on(8, (receive_far, (3, VECTOR)), (last_far, (0,)))
        on(9, (last_far, (3, VECTOR)))
        @pl.when((j < 5) | (j == 6))
        def _():
            y_recv(j + 1, FIRST)
            y_issue(j + 1, PASSED)

        y_recv(j, PASSED)
        permute(j, pl.ds(3 * nb, nb), False)
        on(8, (last_far, (1,)))

        @pl.when((h == 0) & (s < 3))
        def _():
            join(s)


        on(7, (join, (3,)))

        @pl.when(j == 9)
        def _():
            join_part(4, VECTOR)
            finish_vector(4)
            lax.fori_loop(0, HALVES - 1, drain, 0)
            lax.fori_loop(0, 3, drain_panel, 0)
            drain_next()
            for q in range(VECTOR):
                join_part(4, q)

        def multiply(hh, carry):
            product(s, hh)
            return carry

        low = jnp.where(s < 3, h, 0)
        high = jnp.where((s < 3) | (h == 1), h + 1, 0)
        lax.fori_loop(low, high, multiply, 0)

        def start_third(q):
            for c in local_sends(2, q):
                c.start()

        def start_far(q):
            far_send(q).start()

        on(5, (start_next, (2, 3)))
        for done, new in ((2, (4,)), (3, (5,)), (4, (6,)), (5, (7,)), (7, (8, 9))):
            @pl.when(j == done)
            def _():
                for n in new:
                    y_issue(n, FIRST)
                    y_issue(n, SECOND)

        on(0, (start_third, (0, 1)))
        on(1, (start_third, (2, 3)))
        on(4, (start_next, (0, 1)))
        on(7, (start_far, (0, 1, 2, 3)))

        @pl.when((h == 1) & (s < 4))
        def _():
            finish_vector(s)

        on(1, (start_third, (VECTOR,)))
        on(5, (start_next, (VECTOR,)))
        on(7, (start_far, (VECTOR,)))

        @pl.when((h == 0) & (s < 4))
        def _():
            make_hot(s + 1)

        return carry

    lax.fori_loop(0, HALVES, step, 0)
    rhs_ref[...] = rbuf[pl.ds(0, 1), own_cols]

    for i, dcol in enumerate((1, -1, 2)):
        g_copy(i, dcol, 0).wait_send()
    drain(HALVES - 1, 0)
    drain_panel(4, 0)
    for q in range(5):
        far_send(q).wait_send()


def deliver(block_ref, rhs_ref, block_out, rhs_out, sems):
    copies = [
        pltpu.make_async_copy(block_ref, block_out, sems.at[0]),
        pltpu.make_async_copy(rhs_ref, rhs_out, sems.at[1]),
    ]
    for copy in copies:
        copy.start()
    for copy in copies:
        copy.wait()


def shards(interval_blocks, interval_pivots, boundary_pivots, interval_residuals):
    blocks, residuals = interval_blocks[0], interval_residuals[0]
    nb, share = blocks.shape[1], residuals.shape[1]
    vmem = pl.BlockSpec(memory_space=pltpu.VMEM)
    anywhere = pl.BlockSpec(memory_space=pl.ANY)
    interval_rows = jnp.transpose(interval_pivots, (1, 0, 2))
    reduced, rhs = pl.pallas_call(
        body,
        out_shape=(jax.ShapeDtypeStruct((nb, nb), BF), jax.ShapeDtypeStruct((1, share), F32)),
        in_specs=[anywhere] * 4,
        out_specs=(vmem, vmem),
        scratch_shapes=[
            pltpu.VMEM(interval_rows.shape, jnp.int32),
            pltpu.VMEM(boundary_pivots.shape, jnp.int32),
            pltpu.VMEM(residuals.shape, BF),
            pltpu.VMEM((STAGES, nb, 4 * nb), BF),
            pltpu.VMEM((STAGES, 4 * nb, nb), BF),
            pltpu.VMEM((STAGES, 16, 4 * nb), BF),
            pltpu.VMEM((2, 16, nb), BF),
            pltpu.VMEM((nb, nb), BF),
            pltpu.VMEM((16, nb), BF),
            pltpu.VMEM((nb, 4 * nb), BF),
            pltpu.VMEM((2, 4 * nb, 4 * nb), BF),
            pltpu.VMEM((8, 4 * nb), jnp.int32),
            pltpu.VMEM((8, share), F32),
            pltpu.VMEM((8, nb), F32),
            pltpu.VMEM((16, nb), F32),
            pltpu.VMEM((16, nb), F32),
            pltpu.SemaphoreType.DMA((7,)),
            pltpu.SemaphoreType.DMA((3,)),
            pltpu.SemaphoreType.DMA((3,)),
            pltpu.SemaphoreType.DMA((HALVES, 3, 2)),
            pltpu.SemaphoreType.DMA((HALVES, 3, 2)),
            pltpu.SemaphoreType.DMA((STAGES, 4, 5)),
            pltpu.SemaphoreType.DMA((STAGES, 4, 5)),
            pltpu.SemaphoreType.DMA((5,)),
            pltpu.SemaphoreType.DMA((5,)),
            pltpu.SemaphoreType.DMA((STAGES, 2, 5)),
        ],
        compiler_params=pltpu.CompilerParams(
            collective_id=0, has_side_effects=True, vmem_limit_bytes=60 * 2**20
        ),
        name="newton",
    )(blocks, interval_rows, boundary_pivots, residuals)
    reduced, rhs = pl.pallas_call(
        deliver,
        out_shape=(jax.ShapeDtypeStruct((nb, nb), BF), jax.ShapeDtypeStruct((1, share), F32)),
        in_specs=[anywhere] * 2,
        out_specs=(vmem, vmem),
        scratch_shapes=[pltpu.SemaphoreType.DMA((2,))],
        name="deliver",
    )(reduced, rhs)
    return reduced[None], rhs


def solution(mesh):
    placed = (
        P("loop", None, "row", "col"),
        P("loop", None, None),
        P(),
        P("loop", None, ("row", "col")),
    )
    return jax.shard_map(
        shards,
        mesh=mesh,
        in_specs=placed,
        out_specs=(P("loop", "row", "col"), P("loop", ("row", "col"))),
        check_vma=False,
    )
```

```python
import jax
import jax.numpy as jnp
from jax import lax
from jax.experimental import pallas as pl
from jax.experimental.pallas import tpu as pltpu
from jax.sharding import PartitionSpec as P

MESH = pl.DeviceIdType.MESH
BF, F32 = jnp.bfloat16, jnp.float32
NT = (((1,), (1,)), ((), ()))

FIRST, SECOND, PASSED = 0, 1, 2
STAGES, HALVES, VECTOR = 5, 10, 4


def body(w_ref, ipiv_hbm, bpiv_hbm, res_hbm, out_ref, rhs_ref, ipiv_ref, bpiv_ref, res_ref, gath, panel, vecs, own_vec, relay, relay_vec, perm, hot, pivs,
         gsend, gbuf, rbuf, held, load_sem, gs_sem, gr_sem, ys_sem, yr_sem, ps_sem, pr_sem, rs_sem, rr_sem, fs_sem):
    loop, row, col = lax.axis_index("loop"), lax.axis_index("row"), lax.axis_index("col")
    n_loop, n_row, n_col = lax.axis_size("loop"), lax.axis_size("row"), lax.axis_size("col")
    nb = perm.shape[0]
    half, quarter = nb // 2, nb // 4
    share = res_ref.shape[1]
    odd = lax.rem(loop, 2) == 1
    even = lax.rem(loop, 2) == 0
    own_lanes = pl.ds(0, nb)

    def at(dloop=0, row_=None, dcol=0):
        return {
            "loop": lax.rem(loop + dloop + n_loop, n_loop),
            "row": row if row_ is None else row_,
            "col": lax.rem(col + dcol + n_col, n_col),
        }

    sibling = row + 1 - 2 * lax.rem(row, 2)
    across = lax.rem(row + 2, n_row)

    def copy(src, dst, ssem, rsem, dev):
        return pltpu.make_async_remote_copy(
            src_ref=src, dst_ref=dst, send_sem=ssem, recv_sem=rsem, device_id=dev, device_id_type=MESH
        )

    def y_copy(j, k, direction):
        s, h = lax.div(j, 2), lax.rem(j, 2)
        near = 1 + direction
        offset = (direction + (k == SECOND)) % 2 * quarter
        rows = pl.ds(pl.multiple_of(h * half + offset, quarter), quarter)
        near_lanes = pl.ds(near * nb, nb)
        if k == PASSED:
            src, dst = gath.at[s, rows, near_lanes], gath.at[s, rows, pl.ds(3 * nb, nb)]
        else:
            src, dst = gath.at[s, rows, own_lanes], gath.at[s, rows, near_lanes]
        return copy(src, dst, ys_sem.at[j, k, direction], yr_sem.at[j, k, direction], at(dcol=1 - 2 * direction))

    def y_issue(j, k):
        for direction in (0, 1):
            y_copy(j, k, direction).start()

    def y_recv(j, k):
        for direction in (0, 1):
            y_copy(j, k, direction).wait_recv()

    def part(t, slot, q):
        if q == VECTOR:
            return vecs.at[t, :, pl.ds(slot * nb, nb)]
        return panel.at[t, pl.ds(slot * nb + q * quarter, quarter)]

    def own_part(t, q):
        if q == VECTOR:
            return own_vec.at[t - 3]
        return gath.at[t, pl.ds(q * quarter, quarter), own_lanes]

    def p_copy(t, q, src, slot, dev):
        return copy(src, part(t, slot, q), ps_sem.at[t, slot, q], pr_sem.at[t, slot, q], dev)

    def local_sends(t, q):
        return [p_copy(t, q, part(t, 0, q), 1, at(row_=sibling)), p_copy(t, q, part(t, 0, q), 2, at(row_=across))]

    def next_sends(q):
        src = own_part(3, q)
        return [p_copy(3, q, src, 0, at(dloop=1)), p_copy(3, q, src, 2, at(dloop=1, row_=across))]

    def relay_part(q):
        return relay_vec if q == VECTOR else relay.at[pl.ds(q * quarter, quarter)]

    def relay_send(q):
        return copy(own_part(3, q), relay_part(q), rs_sem.at[q], rr_sem.at[q], at(dloop=2))

    def relay_passes(q):
        src = relay_part(q)
        return [p_copy(3, q, src, 0, at(dloop=-1)), p_copy(3, q, src, 2, at(dloop=-1, row_=across))]

    def far_send(q):
        return p_copy(4, q, own_part(4, q), 0, at(dloop=2))

    def to_sibling(t, q, slot):
        return copy(part(t, slot, q), part(t, slot + 1, q), fs_sem.at[t, slot // 2, q], pr_sem.at[t, slot + 1, q], at(row_=sibling))

    def p_recv(t, slot, q):
        p_copy(t, q, part(t, slot, q), slot, at(row_=sibling)).wait_recv()

    def far_forward(t, q):
        p_recv(t, 2, q)
        to_sibling(t, q, 2).start()

    def join_part(t, q):
        p_recv(t, 1, q)
        p_recv(t, 3, q)

    def join(t):
        for q in range(5):
            join_part(t, q)

    def start_next(q):
        @pl.when(even)
        def _():
            for c in next_sends(q):
                c.start()

        @pl.when(odd)
        def _():
            relay_send(q).start()

    def pass_relay(q):
        @pl.when(odd)
        def _():
            relay_send(q).wait_recv()
            for c in relay_passes(q):
                c.start()

    def make_hot(s):
        for slot, dcol in enumerate((0, n_col - 1, 1, 2)):
            start = pl.multiple_of(lax.rem(col + dcol, n_col) * nb, nb)
            q = pivs[pl.ds(s, 1), pl.ds(start, nb)]

            def one(row_slot, carry):
                base = lax.rem(row + 2 * lax.div(row_slot, 2), n_row)
                base = base + (1 - 2 * lax.rem(base, 2)) * lax.rem(row_slot, 2)
                iota = lax.broadcasted_iota(jnp.int16, (nb, nb), 0)
                wanted = jnp.broadcast_to((q - base * nb).astype(jnp.int16), (nb, nb))
                rows = pl.ds(pl.multiple_of(row_slot * nb, nb), nb)
                hot[lax.rem(s, 2), rows, pl.ds(slot * nb, nb)] = jnp.where(iota == wanted, BF(1), BF(0))
                return carry

            lax.fori_loop(0, 4, one, 0)

    def permute(j, lanes, first):
        s, h = lax.div(j, 2), lax.rem(j, 2)
        rows = pl.ds(pl.multiple_of(h * half, half), half)

        def one(part_, carry):
            targets = pl.ds(pl.multiple_of(part_ * 2 * nb, 2 * nb), 2 * nb)
            moved = lax.dot_general(gath[s, rows, lanes], hot[lax.rem(s, 2), targets, lanes], NT, preferred_element_type=F32).astype(BF)
            if first:
                perm[rows, targets] = moved
            else:
                perm[rows, targets] += moved
            return carry

        lax.fori_loop(0, 2, one, 0)

    def product(s, h):
        rows = pl.ds(pl.multiple_of(h * half, half), half)
        value = jnp.dot(perm[rows, :], panel[s], preferred_element_type=F32).astype(BF)

        @pl.when(s == 0)
        def _():
            panel[2, rows, :] = value

        @pl.when((s >= 1) & (s < 4))
        def _():
            gath[s + 1, rows, own_lanes] = value

        @pl.when(s == 4)
        def _():
            out_ref[rows, :] = value

    def finish_vector(s):
        rbuf[...] = lax.dot_general(vecs[s], perm[...], NT, preferred_element_type=F32)

        @pl.when(s < 2)
        def _():
            rbuf[...] += gbuf[pl.ds(2 * s + 1, 1), :]

        @pl.when(s == 0)
        def _():
            vecs[2, :, own_lanes] = rbuf[...].astype(BF)

        @pl.when(s == 1)
        def _():
            held[...] = rbuf[...]

        @pl.when(s == 2)
        def _():
            rbuf[...] += held[...]

        @pl.when(s >= 3)
        def _():
            rbuf[...] += own_vec[s - 3].astype(F32)

        @pl.when((s >= 2) & (s < 4))
        def _():
            own_vec[s - 2] = rbuf[...].astype(BF)

    loads = []
    for s in range(2):
        loads.append(pltpu.make_async_copy(w_ref.at[2 * s + 1], gath.at[s, :, own_lanes], load_sem.at[2 * s]))
        loads.append(pltpu.make_async_copy(w_ref.at[2 * s], panel.at[s, pl.ds(0, nb)], load_sem.at[2 * s + 1]))
    small = [
        pltpu.make_async_copy(src, dst, load_sem.at[4 + i])
        for i, (src, dst) in enumerate(((ipiv_hbm, ipiv_ref), (bpiv_hbm, bpiv_ref), (res_hbm, res_ref)))
    ]
    for load in small + loads:
        load.start()
    barrier = pltpu.get_barrier_semaphore()
    partners = (
        at(dcol=1), at(dcol=-1), at(dcol=2), at(row_=sibling), at(row_=across),
        at(dloop=1), at(dloop=-1), at(dloop=1, row_=across), at(dloop=-1, row_=across), at(dloop=2), at(dloop=-2),
    )
    for partner in partners:
        pl.semaphore_signal(barrier, inc=1, device_id=partner, device_id_type=MESH)
    own_cols = pl.ds(pl.multiple_of(col * share, share), share)
    for load in small:
        load.wait()
    gsend[...] = jnp.zeros_like(gsend)
    gsend[pl.ds(0, 4), :] = res_ref[...].astype(F32)
    gbuf[:, own_cols] = gsend[...]
    for s, interval in enumerate((0, 2, 1)):
        pivs[pl.ds(s, 1), :] = ipiv_ref[interval]
    pivs[pl.ds(3, 1), :] = bpiv_ref[pl.ds(loop, 1), :]
    pivs[pl.ds(4, 1), :] = bpiv_ref[pl.ds(lax.rem(loop + n_loop - 1, n_loop), 1), :]
    for load in loads:
        load.wait()
    pl.semaphore_wait(barrier, len(partners))

    def g_copy(i, dcol, holder):
        cols = pl.ds(pl.multiple_of(lax.rem(col + holder + n_col, n_col) * share, share), share)
        return copy(gsend, gbuf.at[:, cols], gs_sem.at[i], gr_sem.at[i], at(dcol=dcol))

    for j in (0, 1):
        y_issue(j, FIRST)
        y_issue(j, SECOND)
    for i, dcol in enumerate((1, -1, 2)):
        g_copy(i, dcol, 0).start()
    for q in range(4):
        for c in local_sends(0, q):
            c.start()
    make_hot(0)
    for i, dcol in enumerate((-1, 1, 2)):
        g_copy(i, dcol, dcol).wait_recv()
    for s in (0, 1):
        vecs[s, :, own_lanes] = jnp.broadcast_to(gbuf[pl.ds(2 * s, 1), :], (16, nb)).astype(BF)
    for c in local_sends(0, VECTOR):
        c.start()

    def drain(j, carry):
        for k in (FIRST, SECOND, PASSED):
            for direction in (0, 1):
                y_copy(j, k, direction).wait_send()
        return carry

    def drain_panel(t, carry):
        for q in range(5):
            for c in local_sends(t, q):
                c.wait_send()
            to_sibling(t, q, 2).wait_send()
        return carry

    def drain_next():
        for q in range(5):
            for slot in (0, 2):
                to_sibling(3, q, slot).wait_send()
            for c in next_sends(q):
                c.wait_send()

        @pl.when(odd)
        def _():
            for q in range(5):
                relay_send(q).wait_send()

    def step(j, carry):
        s, h = lax.div(j, 2), lax.rem(j, 2)

        def on(number, *actions):
            @pl.when(j == number)
            def _():
                for action, qs in actions:
                    for q in qs:
                        action(q)

        def first_far(q):
            far_forward(0, q)
            for c in local_sends(1, q):
                c.start()

        def second_far(q):
            far_forward(1, q)

        def third_far(q):
            far_forward(2, q)

        def pass_next(q):
            for slot in (0, 2):
                p_recv(3, slot, q)
                to_sibling(3, q, slot).start()

        def receive_far(q):
            p_recv(4, 0, q)
            for c in local_sends(4, q):
                c.start()

        def last_far(q):
            far_forward(4, q)

        @pl.when((j == 0) | (j == 6) | (j == 8))
        def _():
            y_recv(j, FIRST)
            y_issue(j, PASSED)

        on(6, (pass_relay, (1,)), (pass_next, (0,)))

        @pl.when(j == 8)
        def _():
            y_recv(9, FIRST)
            y_issue(9, PASSED)

        on(8, (receive_far, (0,)))

        permute(j, own_lanes, True)
        on(8, (receive_far, (1,)))
        y_recv(j, SECOND)
        for last, new in ((0, 2), (1, 3)):
            @pl.when(j == last)
            def _():
                y_issue(new, FIRST)
                y_issue(new, SECOND)

        on(6, (pass_next, (1,)), (pass_relay, (2,)))
        on(7, (pass_next, (2,)))
        on(8, (receive_far, (2,)))
        on(9, (last_far, (2,)))

        permute(j, pl.ds(nb, 2 * nb), False)
        on(0, (first_far, (0, 1, 2, 3, VECTOR)))
        on(1, (second_far, (0, 1)))
        on(2, (second_far, (2, 3, VECTOR)))
        on(3, (third_far, (0, 1, 2, 3, VECTOR)))
        on(5, (pass_relay, (0,)))
        on(6, (pass_relay, (3, VECTOR)))
        on(7, (pass_next, (3, VECTOR)))
        on(8, (receive_far, (3, VECTOR)), (last_far, (0,)))
        on(9, (last_far, (3, VECTOR)))
        @pl.when((j < 5) | (j == 6))
        def _():
            y_recv(j + 1, FIRST)
            y_issue(j + 1, PASSED)

        y_recv(j, PASSED)
        permute(j, pl.ds(3 * nb, nb), False)
        on(8, (last_far, (1,)))

        @pl.when((h == 0) & (s < 3))
        def _():
            join(s)


        on(7, (join, (3,)))

        @pl.when(j == 9)
        def _():
            join_part(4, VECTOR)
            finish_vector(4)
            lax.fori_loop(0, HALVES - 1, drain, 0)
            lax.fori_loop(0, 3, drain_panel, 0)
            drain_next()
            for q in range(VECTOR):
                join_part(4, q)

        def multiply(hh, carry):
            product(s, hh)
            return carry

        low = jnp.where(s < 3, h, 0)
        high = jnp.where((s < 3) | (h == 1), h + 1, 0)
        lax.fori_loop(low, high, multiply, 0)

        def start_third(q):
            for c in local_sends(2, q):
                c.start()

        def start_far(q):
            far_send(q).start()

        on(5, (start_next, (2, 3)))
        for done, new in ((2, (4,)), (3, (5,)), (4, (6,)), (5, (7,)), (7, (8, 9))):
            @pl.when(j == done)
            def _():
                for k in (FIRST, SECOND):
                    for n in new:
                        y_issue(n, k)

        on(0, (start_third, (0, 1)))
        on(1, (start_third, (2, 3)))
        on(4, (start_next, (0, 1)))
        on(7, (start_far, (0, 1, 2, 3)))

        @pl.when((h == 1) & (s < 4))
        def _():
            finish_vector(s)

        on(1, (start_third, (VECTOR,)))
        on(5, (start_next, (VECTOR,)))
        on(7, (start_far, (VECTOR,)))

        @pl.when((h == 0) & (s < 4))
        def _():
            make_hot(s + 1)

        return carry

    lax.fori_loop(0, HALVES, step, 0)
    rhs_ref[...] = rbuf[pl.ds(0, 1), own_cols]

    for i, dcol in enumerate((1, -1, 2)):
        g_copy(i, dcol, 0).wait_send()
    drain(HALVES - 1, 0)
    drain_panel(4, 0)
    for q in range(5):
        far_send(q).wait_send()


def deliver(block_ref, rhs_ref, block_out, rhs_out, sems):
    copies = [
        pltpu.make_async_copy(block_ref, block_out, sems.at[0]),
        pltpu.make_async_copy(rhs_ref, rhs_out, sems.at[1]),
    ]
    for copy in copies:
        copy.start()
    for copy in copies:
        copy.wait()


def shards(interval_blocks, interval_pivots, boundary_pivots, interval_residuals):
    blocks, residuals = interval_blocks[0], interval_residuals[0]
    nb, share = blocks.shape[1], residuals.shape[1]
    vmem = pl.BlockSpec(memory_space=pltpu.VMEM)
    anywhere = pl.BlockSpec(memory_space=pl.ANY)
    interval_rows = jnp.transpose(interval_pivots, (1, 0, 2))
    reduced, rhs = pl.pallas_call(
        body,
        out_shape=(jax.ShapeDtypeStruct((nb, nb), BF), jax.ShapeDtypeStruct((1, share), F32)),
        in_specs=[anywhere] * 4,
        out_specs=(vmem, vmem),
        scratch_shapes=[
            pltpu.VMEM(interval_rows.shape, jnp.int32),
            pltpu.VMEM(boundary_pivots.shape, jnp.int32),
            pltpu.VMEM(residuals.shape, BF),
            pltpu.VMEM((STAGES, nb, 4 * nb), BF),
            pltpu.VMEM((STAGES, 4 * nb, nb), BF),
            pltpu.VMEM((STAGES, 16, 4 * nb), BF),
            pltpu.VMEM((2, 16, nb), BF),
            pltpu.VMEM((nb, nb), BF),
            pltpu.VMEM((16, nb), BF),
            pltpu.VMEM((nb, 4 * nb), BF),
            pltpu.VMEM((2, 4 * nb, 4 * nb), BF),
            pltpu.VMEM((8, 4 * nb), jnp.int32),
            pltpu.VMEM((8, share), F32),
            pltpu.VMEM((8, nb), F32),
            pltpu.VMEM((16, nb), F32),
            pltpu.VMEM((16, nb), F32),
            pltpu.SemaphoreType.DMA((7,)),
            pltpu.SemaphoreType.DMA((3,)),
            pltpu.SemaphoreType.DMA((3,)),
            pltpu.SemaphoreType.DMA((HALVES, 3, 2)),
            pltpu.SemaphoreType.DMA((HALVES, 3, 2)),
            pltpu.SemaphoreType.DMA((STAGES, 4, 5)),
            pltpu.SemaphoreType.DMA((STAGES, 4, 5)),
            pltpu.SemaphoreType.DMA((5,)),
            pltpu.SemaphoreType.DMA((5,)),
            pltpu.SemaphoreType.DMA((STAGES, 2, 5)),
        ],
        compiler_params=pltpu.CompilerParams(
            collective_id=0, has_side_effects=True, vmem_limit_bytes=60 * 2**20
        ),
        name="newton",
    )(blocks, interval_rows, boundary_pivots, residuals)
    reduced, rhs = pl.pallas_call(
        deliver,
        out_shape=(jax.ShapeDtypeStruct((nb, nb), BF), jax.ShapeDtypeStruct((1, share), F32)),
        in_specs=[anywhere] * 2,
        out_specs=(vmem, vmem),
        scratch_shapes=[pltpu.SemaphoreType.DMA((2,))],
        name="deliver",
    )(reduced, rhs)
    return reduced[None], rhs


def solution(mesh):
    placed = (
        P("loop", None, "row", "col"),
        P("loop", None, None),
        P(),
        P("loop", None, ("row", "col")),
    )
    return jax.shard_map(
        shards,
        mesh=mesh,
        in_specs=placed,
        out_specs=(P("loop", "row", "col"), P("loop", ("row", "col"))),
        check_vma=False,
    )
```
